32 devices in a mesh: row: 4 (over y, core), col: 8 (over z, x).
Axes of the slice: x: 2, y: 2, z: 4, core: 2. Of those that a mesh axis runs over, the one named last changes fastest.
Arguments:
- contribution: float32 [8, 4, 4, 8, 128, 128], P(None, 'row', None, 'col'), may hold values from -6 to 6
- parent_tiles: float32 [16, 4, 8, 8, 128, 128], P(None, 'row', None, 'col'), may hold values from -6 to 6
- row_basis: float32 [8, 4, 64, 128], P(None, 'row'), may hold values from -2.4 to 2.4
- pivot_basis: float32 [8, 4, 64, 2048], P(None, 'row', None, 'col'), may hold values from -0.125 to 0.125
- tile_ranks: int32 [32], replicated, may hold values from 16 to 64, as said below
- block_map: int32 [32], replicated, may hold values from 0 to 63, as said below
- panel_start: int32 [1], replicated, may hold values from 0 to 31
- pivot_inverse: float32 [512, 512], replicated
Outputs:
- updated_parent: float32 [16, 4, 8, 8, 128, 128], P(None, 'row', None, 'col')
The draws below stay inside these ranges and needn't reach their ends.
Inputs may be any that keep to these rules, and one draw needn't show every extreme that they name: `tile_ranks`: multiples of 16; both 16 and 64 occur. `block_map`: child tile row u * 8 + l, for 0 <= l < 8, maps to parent tile row 2 * 8 * u + h_u + l with 0 <= h_u < 8; the 4 values h_u are distinct modulo 4.
All inputs are finite; a program needn't handle non-finite values.
Results may differ from the reference program's by a relative error of at most 0.0003.
Values sent between devices are 32-bit elements; how exact they have to be, the bound alone decides.
A program may use at most 128 MiB of HBM per device.

```python
import jax
import jax.numpy as jnp
from jax import lax

B = 128
P_SIZE = 2048
RMAX = 64
PANEL_T = 4
CT_COL = 4
GRID_R = 4
GRID_C = 8
NTC = 32
CT_ROW = 8
PT_ROW = 16
PT_COL = 8
PW = 512


def draw_block_map(key, part):
    key_perm, key_coin = jax.random.split(jax.random.fold_in(key, 11))
    residues = jax.random.permutation(key_perm, GRID_R)[:CT_COL]
    coins = jax.random.randint(key_coin, (CT_COL,), 0, GRID_C // GRID_R)
    shifts = residues + GRID_R * coins
    blocks = jnp.arange(CT_COL)[:, None]
    within = jnp.arange(GRID_C)[None, :]
    return (2 * GRID_C * blocks + shifts[:, None] + within).reshape(-1).astype(jnp.int32)


def draw_tile_ranks(key, part):
    key_rank, key_place = jax.random.split(jax.random.fold_in(key, 23))
    levels = 16 * jax.random.randint(key_rank, (NTC,), 1, RMAX // 16 + 1)
    order = jax.random.permutation(key_place, NTC)
    levels = levels.at[order[0]].set(RMAX).at[order[1]].set(16)
    return levels.astype(jnp.int32)


def draw_pivot_inverse(key, part):
    key_noise = jax.random.fold_in(key, 37)
    noise = jnp.clip(jax.random.normal(key_noise, (PW, PW), jnp.float32), -4.0, 4.0)
    matrix = jnp.eye(PW, dtype=jnp.float32) + 0.5 * noise / jnp.sqrt(jnp.float32(PW))
    return (matrix / (2.0 * jnp.sqrt(jnp.float32(PW)))).astype(jnp.float32)


def shard_levels(rng, dims, cuts, smallest, top_value):
    gain, own = 1.0, jax.random.fold_in(rng, 6)
    for axis_at, blocks in cuts:
        draws = jnp.exp(jax.random.uniform(jax.random.fold_in(own, axis_at), (blocks,), jnp.float32, smallest / len(cuts), top_value / len(cuts)))
        gain = gain * jnp.repeat(draws, dims[axis_at] // blocks).reshape([-1 if axis == axis_at else 1 for axis in range(len(dims))])
    return gain


def normal_values(stream_key, shape, width, bound, cuts=(), held_as=jnp.bfloat16):
    loudness = shard_levels(stream_key, shape, cuts, -0.22, 0.18) if cuts else 1.0
    array = jax.random.normal(stream_key, shape, jnp.float32) * width * loudness
    return jnp.minimum(jnp.maximum(array, -bound), bound).astype(held_as)


def setup_inputs(seed: int = 0) -> dict:
    splits = jax.random.split(jax.random.key(seed), 9)
    return {
        "contribution": normal_values(splits[0], (CT_ROW, GRID_R, CT_COL, GRID_C, B, B), 1.0, 6.0, ((1, 4), (3, 8)), jnp.float32),
        "parent_tiles": normal_values(splits[1], (PT_ROW, GRID_R, PT_COL, GRID_C, B, B), 1.0, 6.0, ((1, 4), (3, 8)), jnp.float32),
        "row_basis": normal_values(splits[2], (CT_ROW, GRID_R, RMAX, B), 0.4, 2.4, ((1, 4),), jnp.float32),
        "pivot_basis": normal_values(splits[3], (CT_ROW, GRID_R, RMAX, P_SIZE), P_SIZE ** -0.5, 0.125, ((1, 4), (3, 8)), jnp.float32),
        "tile_ranks": draw_tile_ranks(jax.random.fold_in(splits[8], 71), 0),
        "block_map": draw_block_map(jax.random.fold_in(splits[8], 71), 0),
        "panel_start": jax.random.randint(splits[6], (1,), 0, NTC).astype(jnp.int32),
        "pivot_inverse": draw_pivot_inverse(jax.random.fold_in(splits[8], 71), 0),
    }


highest = lax.Precision.HIGHEST


def reference(contribution, parent_tiles, row_basis, pivot_basis, tile_ranks, block_map, panel_start, pivot_inverse):
    child_total = contribution.shape[0] * contribution.shape[1]
    parent_total = parent_tiles.shape[0] * parent_tiles.shape[1]
    tile_size = contribution.shape[4]
    rank_max = row_basis.shape[2]
    kept_cols = (jnp.arange(rank_max, dtype=jnp.int32)[None, :] < tile_ranks[:, None]).astype(jnp.float32)
    bases = row_basis.reshape(child_total, rank_max, tile_size) * kept_cols[:, :, None]
    pivots = pivot_basis.reshape(child_total * rank_max, -1)
    gram = jnp.dot(pivots, pivots.T, precision=highest, preferred_element_type=jnp.float32)
    gram = gram.reshape(child_total, rank_max, child_total, rank_max)
    half_product = jnp.einsum("irx,irju->ixju", bases, gram, precision=highest, preferred_element_type=jnp.float32)
    update = jnp.einsum("ixju,juy->ijxy", half_product, bases, precision=highest, preferred_element_type=jnp.float32)
    tile_index = jnp.arange(child_total, dtype=jnp.int32)
    lower_mask = tile_index[:, None] >= tile_index[None, :]
    blocks = contribution.reshape(child_total, child_total, tile_size, tile_size)
    moved_tiles = jnp.where(lower_mask[:, :, None, None], blocks - update, jnp.float32(0.0))
    parent_grid = parent_tiles.reshape(parent_total, parent_total, tile_size, tile_size)
    assembled = parent_grid.at[block_map[:, None], block_map[None, :]].add(moved_tiles)
    start_col = panel_start[0].astype(jnp.int32)
    panel = lax.dynamic_slice_in_dim(assembled, start_col, PANEL_T, axis=1)
    row_panel = jnp.transpose(panel, (0, 2, 1, 3)).reshape(parent_total, tile_size, PANEL_T * tile_size)
    scaled = jnp.einsum("axp,pq->axq", row_panel, pivot_inverse, precision=highest, preferred_element_type=jnp.float32)
    col_index = jnp.arange(parent_total, dtype=jnp.int32)

    def trailing_row(inputs):
        row_id, current, scaled_row = inputs
        trailing = jnp.einsum("xq,byq->bxy", scaled_row, row_panel, precision=highest, preferred_element_type=jnp.float32)
        window = (row_id >= col_index) & (col_index >= start_col + PANEL_T)
        return jnp.where(window[:, None, None], current - trailing, current)

    result = lax.map(trailing_row, (col_index, assembled, scaled))
    return result.reshape(parent_tiles.shape)
```

```python
import jax
import jax.numpy as jnp
from jax import lax
from jax.experimental import pallas as pl
from jax.experimental.pallas import tpu as pltpu
from jax.sharding import PartitionSpec as P

PANEL_T = 4
f32 = jnp.float32
bf16 = jnp.bfloat16
high = lax.Precision.HIGH


def rotate(x, axis, amount):
    n = lax.axis_size(axis)

    def branch(k):
        pairs = [(d, (d + k) % n) for d in range(n)]
        return (lambda v: v) if k == 0 else (lambda v: lax.ppermute(v, axis, pairs))

    return lax.switch(amount, [branch(k) for k in range(n)], x)


def gather_ring(x, axis):
    return lax.all_gather(x, axis, axis=0, tiled=False)


def split(x):
    top = x.astype(bf16)
    return top, (x - top.astype(f32)).astype(bf16)


def split_outside(x):
    top = lax.reduce_precision(x, exponent_bits=8, mantissa_bits=7)
    return top.astype(bf16), (x - top).astype(bf16)


def dot3(a, b, dims):
    (ah, al), (bh, bl) = a, b
    one = lambda p, q: lax.dot_general(p, q, (dims, ((), ())), preferred_element_type=f32)
    return one(ah, bh) + (one(ah, bl) + one(al, bh))


def final_kernel(table, parent, payload, panel, inv_top, inv_low, col_top, col_low, out):
    row = pl.program_id(0)
    bcols = parent.shape[2]
    tile = parent.shape[4]
    blocks = payload.shape[0]
    row_panel = jnp.concatenate([panel[0, 0, m, 0] for m in range(panel.shape[2])], axis=1)
    scaled = dot3(split(row_panel), (inv_top[...], inv_low[...]), ((1,), (0,)))
    trailing = dot3(split(scaled), (col_top[...], col_low[...]), ((1,), (1,)))
    big_row = table[0, 0] + row * table[0, 1]
    place = table[1, row]
    from_row = jnp.maximum(place, 0)
    for b in range(bcols):
        big_col = table[0, 2] + b * table[0, 3]
        s = b // (bcols // blocks)
        hit = (place >= 0) & (table[2, b] > 0)
        active = (big_row >= big_col) & (big_col >= table[0, 4])
        base = parent[0, 0, b, 0] + jnp.where(hit, payload[s, from_row], 0.0)
        out[0, 0, b, 0] = base - jnp.where(active, trailing[:, b * tile : (b + 1) * tile], 0.0)


def finish(table, parent, payload, panel, inv, cols):
    rows, _, bcols, _, tile, _ = parent.shape
    parities, subs, width, piece = panel.shape[:4]
    whole = lambda a: pl.BlockSpec(a.shape, lambda i, t: (0,) * a.ndim)
    big = pl.BlockSpec((1, 1, bcols, 1, tile, tile), lambda i, t: (i, 0, 0, 0, 0, 0))
    picked = pl.BlockSpec(
        (1, 1, width, 1, tile, tile),
        lambda i, t: (i % parities, i // parities // piece, 0, i // parities % piece, 0, 0),
    )
    flops = 6 * rows * tile * width * tile * (width + bcols) * tile
    return pl.pallas_call(
        final_kernel,
        grid_spec=pltpu.PrefetchScalarGridSpec(
            num_scalar_prefetch=1,
            grid=(rows,),
            in_specs=[big, whole(payload), picked, whole(inv[0]), whole(inv[1]), whole(cols[0]), whole(cols[1])],
            out_specs=big,
        ),
        out_shape=jax.ShapeDtypeStruct(parent.shape, f32),
        cost_estimate=pl.CostEstimate(flops=flops, bytes_accessed=10 * parent.size, transcendentals=0),
    )(table, parent, payload, panel, *inv, *cols)


def per_device(
    contribution,
    parent_tiles,
    row_basis,
    pivot_basis,
    tile_ranks,
    block_map,
    panel_start,
    pivot_inverse,
):
    R = lax.axis_size("row")
    C = lax.axis_size("col")
    my_row = lax.axis_index("row")
    my_col = lax.axis_index("col")
    T, S = contribution.shape[0], contribution.shape[2]
    tile = contribution.shape[4]
    rows, bcols = parent_tiles.shape[0], parent_tiles.shape[2]
    rank = row_basis.shape[2]
    width = pivot_basis.shape[3]
    per = C // R
    span = rows // S
    shift = [block_map[u * C] - 2 * u * C for u in range(S)]
    src_row = [(my_row - shift[u]) % R for u in range(S)]
    src_col = [(my_col - shift[s]) % C for s in range(S)]

    child = contribution[:, 0, :, 0]
    by_row = [rotate(child[u * per : (u + 1) * per, : u + 1], "row", shift[u] % R) for u in range(S)]
    moved = [
        rotate(jnp.concatenate([by_row[u][:, s] for u in range(s, S)], axis=0), "col", shift[s])
        for s in range(S)
    ]

    factors = jnp.concatenate([pivot_basis[:, 0], row_basis[:, 0]], axis=2)
    everyone = gather_ring(factors, "row")
    pivots = everyone[..., :width]
    limits = tile_ranks.reshape(T, R).T
    kept = jnp.arange(rank, dtype=jnp.int32)[None, None, :] < limits[:, :, None]
    bases = everyone[..., width:] * kept[..., None].astype(f32)

    def of_rows(stack, u):
        return lax.dynamic_index_in_dim(stack, src_row[u], axis=0, keepdims=False)[u * per : (u + 1) * per]

    pivot_rows = [of_rows(pivots, u).reshape(per * rank, width) for u in range(S)]
    basis_rows = [of_rows(bases, u) for u in range(S)]
    flat_bases = jnp.swapaxes(bases, 0, 1).reshape(S, C, rank, tile)
    flat_pivots = jnp.swapaxes(pivots, 0, 1).reshape(S, C, rank, width)
    partial = []
    for s in range(S):
        mine = jnp.concatenate(pivot_rows[s:], axis=0)
        theirs = jnp.roll(flat_pivots[s], shift[s], axis=0)
        partial.append(jnp.einsum("cqp,mp->cqm", theirs, mine, precision=high, preferred_element_type=f32))
    partial = jnp.concatenate(partial, axis=2)
    weights = lax.psum_scatter(partial, "col", scatter_dimension=0, tiled=True)[0]

    payload, at = [], 0
    for s in range(S):
        size = (S - s) * per * rank
        basis_col = lax.dynamic_index_in_dim(flat_bases[s], src_col[s], axis=0, keepdims=False)
        half = jnp.einsum("qm,qy->my", weights[:, at : at + size], basis_col, precision=high, preferred_element_type=f32)
        at += size
        half = half.reshape((S - s) * per, rank, tile)
        left = jnp.concatenate(basis_rows[s:], axis=0)
        update = jnp.einsum("trx,try->txy", left, half, precision=high, preferred_element_type=f32)
        i = jnp.stack([(u * per + p) * R + src_row[u] for u in range(s, S) for p in range(per)])
        j = s * C + src_col[s]
        tiles = jnp.where((i >= j)[:, None, None], moved[s] - update, 0.0)
        payload.append(jnp.concatenate([jnp.zeros((s * per, tile, tile), f32), tiles], axis=0))
    payload = jnp.stack(payload)

    first_row = jnp.stack([(2 * u * C + shift[u] + src_row[u]) // R for u in range(S)])
    a = jnp.arange(rows, dtype=jnp.int32)
    u_of = a // span
    p_of = a - first_row[u_of]
    place = jnp.where((p_of >= 0) & (p_of < per), u_of * per + p_of, -1).astype(jnp.int32)
    target_col = jnp.stack([(2 * s * C + shift[s] + src_col[s]) // C for s in range(S)])
    b = jnp.arange(bcols, dtype=jnp.int32)
    col_hit = (target_col[b // (bcols // S)] == b).astype(jnp.int32)

    start = panel_start[0]
    owned = (my_col - start) % C < PANEL_T
    own_b = jnp.minimum((start + (my_col - start) % C) // C, bcols - 1)
    column = lax.dynamic_index_in_dim(parent_tiles[:, 0, :, 0], own_b, axis=1, keepdims=False)
    extra = lax.dynamic_index_in_dim(payload, own_b // (bcols // S), axis=0, keepdims=False)
    extra = extra.reshape(S, per, tile, tile)
    grouped = place.reshape(S, span)
    spread = jnp.zeros((S, span, tile, tile), f32)
    for p in range(per):
        sel = (grouped == jnp.arange(S, dtype=jnp.int32)[:, None] * per + p)[:, :, None, None]
        spread = spread + jnp.where(sel, extra[:, p][:, None], 0.0)
    hit = lax.dynamic_index_in_dim(col_hit, own_b, axis=0, keepdims=False) > 0
    column = column + jnp.where(hit, spread.reshape(rows, tile, tile), 0.0)
    subs = R // PANEL_T
    piece = rows // per // subs
    pieces = column.reshape(subs, piece, per, tile, tile)
    pieces = jnp.moveaxis(pieces, 2, 0).reshape(per * subs, piece, tile, tile)
    members = C // PANEL_T
    my_member = my_col // PANEL_T
    held = lax.dynamic_index_in_dim(pieces, my_member, axis=0, keepdims=False)
    for k in range(1, members):
        gone = lax.dynamic_index_in_dim(pieces, (my_member + k) % members, axis=0, keepdims=False)
        came = lax.ppermute(gone, "col", [(d, (d + PANEL_T * k) % C) for d in range(C)])
        theirs = (my_col - PANEL_T * k - start) % C < PANEL_T
        held = jnp.where(theirs, came, held)
    panel = gather_ring(held, "col").reshape(per, subs, PANEL_T, piece, tile, tile)
    cols = lax.dynamic_index_in_dim(panel, my_col // R, axis=0, keepdims=False)
    cols = lax.psum(jnp.where(my_row == my_col % R, cols, 0.0), "row")
    cols = jnp.transpose(cols, (0, 2, 3, 1, 4)).reshape(bcols * tile, PANEL_T * tile)
    inverse = pivot_inverse.reshape(PANEL_T, tile, PANEL_T, tile)
    inverse = jnp.roll(inverse, (start % PANEL_T, start % PANEL_T), axis=(0, 2))
    inverse = inverse.reshape(PANEL_T * tile, PANEL_T * tile)
    scalars = jnp.stack([my_row, R + 0 * my_row, my_col, C + 0 * my_row, start + PANEL_T]).astype(jnp.int32)
    pad = lambda v: jnp.concatenate([v, jnp.zeros((rows - v.shape[0],), jnp.int32)])
    table = jnp.stack([pad(scalars), place, pad(col_hit)])
    return finish(table, parent_tiles, payload, panel, split_outside(inverse), split_outside(cols))


def solution(mesh):
    placed = (
        P(None, "row", None, "col", None, None),
        P(None, "row", None, "col", None, None),
        P(None, "row", None, None),
        P(None, "row", None, "col"),
        P(),
        P(),
        P(),
        P(),
    )
    return jax.shard_map(
        per_device,
        mesh=mesh,
        in_specs=placed,
        out_specs=P(None, "row", None, "col", None, None),
        check_vma=False,
    )
```

```python
import jax
import jax.numpy as jnp
from jax import lax
from jax.experimental import pallas as pl
from jax.experimental.pallas import tpu as pltpu
from jax.sharding import PartitionSpec as P

PANEL_T = 4
f32 = jnp.float32
bf16 = jnp.bfloat16
high = lax.Precision.HIGH


def rotate(x, axis, amount):
    n = lax.axis_size(axis)

    def branch(k):
        pairs = [(d, (d + k) % n) for d in range(n)]
        return (lambda v: v) if k == 0 else (lambda v: lax.ppermute(v, axis, pairs))

    return lax.switch(amount, [branch(k) for k in range(n)], x)


def gather_ring(x, axis):
    return lax.all_gather(x, axis, axis=0, tiled=False)


def split(x):
    top = x.astype(bf16)
    return top, (x - top.astype(f32)).astype(bf16)


def split_outside(x):
    top = lax.reduce_precision(x, exponent_bits=8, mantissa_bits=7)
    return top.astype(bf16), (x - top).astype(bf16)


def dot3(a, b, dims):
    (ah, al), (bh, bl) = a, b
    one = lambda p, q: lax.dot_general(p, q, (dims, ((), ())), preferred_element_type=f32)
    return one(ah, bh) + (one(ah, bl) + one(al, bh))


def ring_place(p, n):
    return jnp.where(p < n // 2, 2 * p, 2 * (n - 1 - p) + 1)


def panel_kernel(held, panel, cols, send, recv, own_sem, cross_send, cross_recv, relay_send):
    R, n = lax.axis_size("row"), lax.axis_size("col")
    my_row, me = lax.axis_index("row"), lax.axis_index("col")
    half = held.shape[0] // 2
    pos = jnp.where(me % 2 == 0, me // 2, n - 1 - me // 2)
    right = ring_place((pos + 1) % n, n)
    left = ring_place((pos + n - 1) % n, n)
    root = me % R
    is_root = my_row == root
    mesh_id = pl.DeviceIdType.MESH

    barrier = pltpu.get_barrier_semaphore()
    for side in (left, right):
        pl.semaphore_signal(barrier, inc=1, device_id={"col": side}, device_id_type=mesh_id)
    for k in range(1, R):
        pl.semaphore_signal(barrier, inc=1, device_id={"row": (my_row + k) % R}, device_id_type=mesh_id)
    pl.semaphore_wait(barrier, R + 1)

    chunk = lambda h: pl.ds(h * half, half)
    own = pltpu.make_async_copy(held, panel.at[me], own_sem)
    own.start()

    def block(side, k):
        return ring_place((pos - k + n) % n if side == 0 else (pos + k) % n, n)

    def step(side, k, h):
        d = block(side, k)
        src = held.at[chunk(h)] if k == 0 else panel.at[d, chunk(h)]
        return pltpu.make_async_remote_copy(
            src, panel.at[d, chunk(h)], send.at[side, k, h], recv.at[side, k, h],
            device_id={"col": right if side == 0 else left}, device_id_type=mesh_id)

    def arrival(side, k, h):
        d = block(side, k + 1)
        return pltpu.make_async_remote_copy(
            panel.at[d, chunk(h)], panel.at[d, chunk(h)], send.at[side, k, h], recv.at[side, k, h],
            device_id={"col": right if side == 0 else left}, device_id_type=mesh_id)

    def cross(m, h, o):
        if o == 0:
            to = my_row + 1 - 2 * (my_row % 2)
        else:
            core = my_row % 2 if h == 0 else 1 - my_row % 2
            to = (my_row // 2 + o) % (R // 2) * 2 + core
        src = panel.at[me // R * R + m, chunk(h)]
        return pltpu.make_async_remote_copy(
            src, cols.at[m, chunk(h)], cross_send.at[m, h, o], cross_recv.at[m, h],
            device_id={"row": to}, device_id_type=mesh_id)

    def forward(d, h, ready=True):
        @pl.when(is_root & (d // R == me // R))
        def _():
            for o in range(1, R // 2):
                cross(d % R, h, o).start()
            cross(d % R, h, 0).start()

    last = n // 2 - 1
    used = [(side, k, h) for k in range(n // 2) for h in range(2) for side in range(2) if k < last or h == side]
    for side, k, h in used:
        if k > 0:
            arrival(side, k - 1, h).wait_recv()
        step(side, k, h).start()
        if k > 0:
            forward(block(side, k), h)
        elif side == 0 and h == 1:
            own.wait()
            forward(me, 0)
            forward(me, 1)
    for side in range(2):
        arrival(side, last - 1, 1 - side).wait_recv()
        forward(block(side, last), 1 - side)
    for side in range(2):
        arrival(side, last, side).wait_recv()
        forward(block(side, last + 1), side)

    @pl.when(is_root)
    def _():
        for m in range(R):
            for h in range(2):
                for o in range(R // 2):
                    cross(m, h, o).wait_send()

    def relay(m, h):
        to = my_row + 1 - 2 * (my_row % 2)
        return pltpu.make_async_remote_copy(
            cols.at[m, chunk(h)], cols.at[m, chunk(h)], relay_send.at[m], cross_recv.at[m, h],
            device_id={"row": to}, device_id_type=mesh_id)

    @pl.when(~is_root & (my_row // 2 == root // 2))
    def _():
        for m in range(R):
            for h in range(2):
                relay(m, h).wait_recv()

    for mine in range(2):
        @pl.when((my_row // 2 != root // 2) & ((my_row + root) % 2 == mine))
        def _():
            for m in range(R):
                relay(m, mine).wait_recv()
                relay(m, mine).start()
            for m in range(R):
                relay(m, 1 - mine).wait_recv()
            for m in range(R):
                relay(m, mine).wait_send()

    for side, k, h in used:
        step(side, k, h).wait_send()


def gather_panel(held):
    R, n = lax.axis_size("row"), lax.axis_size("col")
    dma = pltpu.SemaphoreType.DMA
    anywhere = pl.BlockSpec(memory_space=pl.ANY)
    return pl.pallas_call(
        panel_kernel,
        in_specs=[pl.BlockSpec(memory_space=pltpu.VMEM)],
        out_specs=(anywhere, anywhere),
        out_shape=(jax.ShapeDtypeStruct((n,) + held.shape, f32), jax.ShapeDtypeStruct((R,) + held.shape, f32)),
        scratch_shapes=[dma((2, n // 2, 2)), dma((2, n // 2, 2)), dma, dma((R, 2, R // 2)), dma((R, 2)), dma((R,))],
        compiler_params=pltpu.CompilerParams(collective_id=1, has_side_effects=True),
    )(held)


def final_kernel(table, parent, payload, panel, inv_top, inv_low, col_top, col_low, out, high_part, low_part):
    step = pl.program_id(0)
    per, bcols = parent.shape[0], parent.shape[2]
    tile = parent.shape[4]
    blocks = payload.shape[0]
    group = bcols // blocks
    first_active = table[0, 4]
    big_rows = [table[0, 0] + (step * per + p) * table[0, 1] for p in range(per)]
    big_cols = [table[0, 2] + b * table[0, 3] for b in range(bcols)]

    for b in range(bcols):
        for p in range(per):
            place = table[1, step * per + p]
            hit = (place >= 0) & (table[2, b] > 0)
            out[p, 0, b, 0] = parent[p, 0, b, 0]

            @pl.when(hit)
            def _():
                out[p, 0, b, 0] = parent[p, 0, b, 0] + payload[b // group, jnp.maximum(place, 0)]

    @pl.when(big_rows[-1] >= first_active)
    def _():
        stacked = [jnp.concatenate([panel[p, 0, m, 0] for m in range(panel.shape[2])], axis=1) for p in range(per)]
        scaled = dot3(split(jnp.concatenate(stacked, axis=0)), (inv_top[...], inv_low[...]), ((1,), (0,)))
        top, low = split(scaled)
        high_part[...] = top
        low_part[...] = low
        for g in range(blocks):
            @pl.when((big_rows[-1] >= big_cols[g * group]) & (big_cols[g * group + group - 1] >= first_active))
            def _():
                at = pl.ds(g * group * tile, group * tile)
                trailing = dot3((high_part[...], low_part[...]), (col_top[at, :], col_low[at, :]), ((1,), (1,)))
                for q in range(group):
                    b = g * group + q
                    for p in range(per):
                        active = (big_rows[p] >= big_cols[b]) & (big_cols[b] >= first_active)
                        part = trailing[p * tile : (p + 1) * tile, q * tile : (q + 1) * tile]
                        out[p, 0, b, 0] = out[p, 0, b, 0] - jnp.where(active, part, 0.0)


def finish(table, parent, payload, panel, inv, cols):
    rows, _, bcols, _, tile, _ = parent.shape
    per, subs, width, piece = panel.shape[:4]
    whole = lambda a: pl.BlockSpec(a.shape, lambda i, t: (0,) * a.ndim)
    big = pl.BlockSpec((per, 1, bcols, 1, tile, tile), lambda i, t: (i, 0, 0, 0, 0, 0))
    picked = pl.BlockSpec(
        (per, 1, width, 1, tile, tile), lambda i, t: (0, i // piece, 0, i % piece, 0, 0)
    )
    flops = 6 * rows * tile * width * tile * (width + bcols) * tile
    return pl.pallas_call(
        final_kernel,
        grid_spec=pltpu.PrefetchScalarGridSpec(
            num_scalar_prefetch=1,
            grid=(rows // per,),
            in_specs=[big, whole(payload), picked, whole(inv[0]), whole(inv[1]), whole(cols[0]), whole(cols[1])],
            out_specs=big,
            scratch_shapes=[pltpu.VMEM((per * tile, width * tile), bf16)] * 2,
        ),
        out_shape=jax.ShapeDtypeStruct(parent.shape, f32),
        cost_estimate=pl.CostEstimate(flops=flops, bytes_accessed=10 * parent.size, transcendentals=0),
    )(table, parent, payload, panel, *inv, *cols)


def per_device(
    contribution,
    parent_tiles,
    row_basis,
    pivot_basis,
    tile_ranks,
    block_map,
    panel_start,
    pivot_inverse,
):
    R = lax.axis_size("row")
    C = lax.axis_size("col")
    my_row = lax.axis_index("row")
    my_col = lax.axis_index("col")
    T, S = contribution.shape[0], contribution.shape[2]
    tile = contribution.shape[4]
    rows, bcols = parent_tiles.shape[0], parent_tiles.shape[2]
    rank = row_basis.shape[2]
    width = pivot_basis.shape[3]
    per = C // R
    span = rows // S
    shift = [block_map[u * C] - 2 * u * C for u in range(S)]
    src_row = [(my_row - shift[u]) % R for u in range(S)]
    src_col = [(my_col - shift[s]) % C for s in range(S)]

    child = contribution[:, 0, :, 0]
    by_row = [rotate(child[u * per : (u + 1) * per, : u + 1], "row", shift[u] % R) for u in range(S)]

    factors = jnp.concatenate([pivot_basis[:, 0], row_basis[:, 0]], axis=2)
    everyone = gather_ring(factors, "row")
    everyone, by_row = lax.optimization_barrier((everyone, by_row))
    moved = [
        rotate(jnp.concatenate([by_row[u][:, s] for u in range(s, S)], axis=0), "col", shift[s])
        for s in range(S)
    ]
    pivots = everyone[..., :width]
    limits = tile_ranks.reshape(T, R).T
    kept = jnp.arange(rank, dtype=jnp.int32)[None, None, :] < limits[:, :, None]
    bases = everyone[..., width:] * kept[..., None].astype(f32)

    def of_rows(stack, u):
        return lax.dynamic_index_in_dim(stack, src_row[u], axis=0, keepdims=False)[u * per : (u + 1) * per]

    pivot_rows = [of_rows(pivots, u).reshape(per * rank, width) for u in range(S)]
    basis_rows = [of_rows(bases, u) for u in range(S)]
    flat_bases = jnp.swapaxes(bases, 0, 1).reshape(S, C, rank, tile)
    flat_pivots = jnp.swapaxes(pivots, 0, 1).reshape(S, C, rank, width)
    partial = []
    for s in range(S):
        mine = jnp.concatenate(pivot_rows[s:], axis=0)
        theirs = jnp.roll(flat_pivots[s], shift[s], axis=0)
        partial.append(jnp.einsum("cqp,mp->cqm", theirs, mine, precision=high, preferred_element_type=f32))
    partial = jnp.concatenate(partial, axis=2)
    weights = lax.psum_scatter(partial, "col", scatter_dimension=0, tiled=True)[0]

    payload, at = [], 0
    for s in range(S):
        size = (S - s) * per * rank
        basis_col = lax.dynamic_index_in_dim(flat_bases[s], src_col[s], axis=0, keepdims=False)
        half = jnp.einsum("qm,qy->my", weights[:, at : at + size], basis_col, precision=high, preferred_element_type=f32)
        at += size
        half = half.reshape((S - s) * per, rank, tile)
        left = jnp.concatenate(basis_rows[s:], axis=0)
        update = jnp.einsum("trx,try->txy", left, half, precision=high, preferred_element_type=f32)
        i = jnp.stack([(u * per + p) * R + src_row[u] for u in range(s, S) for p in range(per)])
        j = s * C + src_col[s]
        tiles = jnp.where((i >= j)[:, None, None], moved[s] - update, 0.0)
        payload.append(jnp.concatenate([jnp.zeros((s * per, tile, tile), f32), tiles], axis=0))
    payload = jnp.stack(payload)

    first_row = jnp.stack([(2 * u * C + shift[u] + src_row[u]) // R for u in range(S)])
    a = jnp.arange(rows, dtype=jnp.int32)
    u_of = a // span
    p_of = a - first_row[u_of]
    place = jnp.where((p_of >= 0) & (p_of < per), u_of * per + p_of, -1).astype(jnp.int32)
    target_col = jnp.stack([(2 * s * C + shift[s] + src_col[s]) // C for s in range(S)])
    b = jnp.arange(bcols, dtype=jnp.int32)
    col_hit = (target_col[b // (bcols // S)] == b).astype(jnp.int32)

    start = panel_start[0]
    owned = (my_col - start) % C < PANEL_T
    own_b = jnp.minimum((start + (my_col - start) % C) // C, bcols - 1)
    column = lax.dynamic_index_in_dim(parent_tiles[:, 0, :, 0], own_b, axis=1, keepdims=False)
    extra = lax.dynamic_index_in_dim(payload, own_b // (bcols // S), axis=0, keepdims=False)
    extra = extra.reshape(S, per, tile, tile)
    grouped = place.reshape(S, span)
    spread = jnp.zeros((S, span, tile, tile), f32)
    for p in range(per):
        sel = (grouped == jnp.arange(S, dtype=jnp.int32)[:, None] * per + p)[:, :, None, None]
        spread = spread + jnp.where(sel, extra[:, p][:, None], 0.0)
    hit = lax.dynamic_index_in_dim(col_hit, own_b, axis=0, keepdims=False) > 0
    column = column + jnp.where(hit, spread.reshape(rows, tile, tile), 0.0)
    subs = R // PANEL_T
    piece = rows // per // subs
    pieces = column.reshape(subs, piece, per, tile, tile)
    pieces = jnp.moveaxis(pieces, 2, 0).reshape(per * subs, piece, tile, tile)
    members = C // PANEL_T
    my_member = my_col // PANEL_T
    held = lax.dynamic_index_in_dim(pieces, my_member, axis=0, keepdims=False)
    for k in range(1, members):
        gone = lax.dynamic_index_in_dim(pieces, (my_member + k) % members, axis=0, keepdims=False)
        came = lax.ppermute(gone, "col", [(d, (d + PANEL_T * k) % C) for d in range(C)])
        theirs = (my_col - PANEL_T * k - start) % C < PANEL_T
        held = jnp.where(theirs, came, held)
    panel, cols = gather_panel(held)
    panel = panel.reshape(per, subs, PANEL_T, piece, tile, tile)
    local = lax.dynamic_index_in_dim(panel, my_col // R, axis=0, keepdims=False)
    cols = jnp.where(my_row == my_col % R, local, cols.reshape(local.shape))
    cols = jnp.transpose(cols, (0, 2, 3, 1, 4)).reshape(bcols * tile, PANEL_T * tile)
    inverse = pivot_inverse.reshape(PANEL_T, tile, PANEL_T, tile)
    inverse = jnp.roll(inverse, (start % PANEL_T, start % PANEL_T), axis=(0, 2))
    inverse = inverse.reshape(PANEL_T * tile, PANEL_T * tile)
    scalars = jnp.stack([my_row, R + 0 * my_row, my_col, C + 0 * my_row, start + PANEL_T]).astype(jnp.int32)
    pad = lambda v: jnp.concatenate([v, jnp.zeros((rows - v.shape[0],), jnp.int32)])
    table = jnp.stack([pad(scalars), place, pad(col_hit)])
    return finish(table, parent_tiles, payload, panel, split_outside(inverse), split_outside(cols))


def solution(mesh):
    placed = (
        P(None, "row", None, "col", None, None),
        P(None, "row", None, "col", None, None),
        P(None, "row", None, None),
        P(None, "row", None, "col"),
        P(),
        P(),
        P(),
        P(),
    )
    return jax.shard_map(
        per_device,
        mesh=mesh,
        in_specs=placed,
        out_specs=P(None, "row", None, "col", None, None),
        check_vma=False,
    )
```

```python
import jax
import jax.numpy as jnp
from jax import lax
from jax.experimental import pallas as pl
from jax.experimental.pallas import tpu as pltpu
from jax.sharding import PartitionSpec as P

PANEL_T = 4
f32 = jnp.float32
bf16 = jnp.bfloat16
high = lax.Precision.HIGH


def rotate(x, axis, amount):
    n = lax.axis_size(axis)

    def branch(k):
        pairs = [(d, (d + k) % n) for d in range(n)]
        return (lambda v: v) if k == 0 else (lambda v: lax.ppermute(v, axis, pairs))

    return lax.switch(amount, [branch(k) for k in range(n)], x)


def gather_ring(x, axis):
    return lax.all_gather(x, axis, axis=0, tiled=False)


def split(x):
    top = x.astype(bf16)
    return top, (x - top.astype(f32)).astype(bf16)


def split_outside(x):
    top = lax.reduce_precision(x, exponent_bits=8, mantissa_bits=7)
    return top.astype(bf16), (x - top).astype(bf16)


def dot3(a, b, dims):
    (ah, al), (bh, bl) = a, b
    one = lambda p, q: lax.dot_general(p, q, (dims, ((), ())), preferred_element_type=f32)
    return one(ah, bh) + (one(ah, bl) + one(al, bh))


def ring_place(p, n):
    return jnp.where(p < n // 2, 2 * p, 2 * (n - 1 - p) + 1)


def panel_kernel(held, panel, cols, send, recv, own_sem, cross_send, cross_recv, relay_send):
    R, n = lax.axis_size("row"), lax.axis_size("col")
    my_row, me = lax.axis_index("row"), lax.axis_index("col")
    half = held.shape[0] // 2
    pos = jnp.where(me % 2 == 0, me // 2, n - 1 - me // 2)
    right = ring_place((pos + 1) % n, n)
    left = ring_place((pos + n - 1) % n, n)
    root = me % R
    is_root = my_row == root
    mesh_id = pl.DeviceIdType.MESH

    barrier = pltpu.get_barrier_semaphore()
    for side in (left, right):
        pl.semaphore_signal(barrier, inc=1, device_id={"col": side}, device_id_type=mesh_id)
    for k in range(1, R):
        pl.semaphore_signal(barrier, inc=1, device_id={"row": (my_row + k) % R}, device_id_type=mesh_id)
    pl.semaphore_wait(barrier, R + 1)

    chunk = lambda h: pl.ds(h * half, half)
    own = pltpu.make_async_copy(held, panel.at[me], own_sem)
    own.start()

    def block(side, k):
        return ring_place((pos - k + n) % n if side == 0 else (pos + k) % n, n)

    def step(side, k, h):
        d = block(side, k)
        src = held.at[chunk(h)] if k == 0 else panel.at[d, chunk(h)]
        return pltpu.make_async_remote_copy(
            src, panel.at[d, chunk(h)], send.at[side, k, h], recv.at[side, k, h],
            device_id={"col": right if side == 0 else left}, device_id_type=mesh_id)

    def arrival(side, k, h):
        d = block(side, k + 1)
        return pltpu.make_async_remote_copy(
            panel.at[d, chunk(h)], panel.at[d, chunk(h)], send.at[side, k, h], recv.at[side, k, h],
            device_id={"col": right if side == 0 else left}, device_id_type=mesh_id)

    def cross(m, h, o):
        if o == 0:
            to = my_row + 1 - 2 * (my_row % 2)
        else:
            core = my_row % 2 if h == 0 else 1 - my_row % 2
            to = (my_row // 2 + o) % (R // 2) * 2 + core
        src = panel.at[me // R * R + m, chunk(h)]
        return pltpu.make_async_remote_copy(
            src, cols.at[m, chunk(h)], cross_send.at[m, h, o], cross_recv.at[m, h],
            device_id={"row": to}, device_id_type=mesh_id)

    def forward(d, h, ready=True):
        @pl.when(is_root & (d // R == me // R))
        def _():
            for o in range(1, R // 2):
                cross(d % R, h, o).start()
            cross(d % R, h, 0).start()

    last = n // 2 - 1
    used = [(side, k, h) for k in range(n // 2) for h in range(2) for side in range(2) if k < last or h == side]
    for side, k, h in used:
        if k > 0:
            arrival(side, k - 1, h).wait_recv()
        step(side, k, h).start()
        if k > 0:
            forward(block(side, k), h)
        elif side == 0 and h == 1:
            own.wait()
            forward(me, 0)
            forward(me, 1)
    for side in range(2):
        arrival(side, last - 1, 1 - side).wait_recv()
        forward(block(side, last), 1 - side)
    for side in range(2):
        arrival(side, last, side).wait_recv()
        forward(block(side, last + 1), side)

    @pl.when(is_root)
    def _():
        for m in range(R):
            for h in range(2):
                for o in range(R // 2):
                    cross(m, h, o).wait_send()

    def relay(m, h):
        to = my_row + 1 - 2 * (my_row % 2)
        return pltpu.make_async_remote_copy(
            cols.at[m, chunk(h)], cols.at[m, chunk(h)], relay_send.at[m], cross_recv.at[m, h],
            device_id={"row": to}, device_id_type=mesh_id)

    @pl.when(~is_root & (my_row // 2 == root // 2))
    def _():
        for m in range(R):
            for h in range(2):
                relay(m, h).wait_recv()

    for mine in range(2):
        @pl.when((my_row // 2 != root // 2) & ((my_row + root) % 2 == mine))
        def _():
            for m in range(R):
                relay(m, mine).wait_recv()
                relay(m, mine).start()
            for m in range(R):
                relay(m, 1 - mine).wait_recv()
            for m in range(R):
                relay(m, mine).wait_send()

    for side, k, h in used:
        step(side, k, h).wait_send()


def gather_panel(held):
    R, n = lax.axis_size("row"), lax.axis_size("col")
    dma = pltpu.SemaphoreType.DMA
    anywhere = pl.BlockSpec(memory_space=pl.ANY)
    return pl.pallas_call(
        panel_kernel,
        in_specs=[pl.BlockSpec(memory_space=pltpu.VMEM)],
        out_specs=(anywhere, anywhere),
        out_shape=(jax.ShapeDtypeStruct((n,) + held.shape, f32), jax.ShapeDtypeStruct((R,) + held.shape, f32)),
        scratch_shapes=[dma((2, n // 2, 2)), dma((2, n // 2, 2)), dma, dma((R, 2, R // 2)), dma((R, 2)), dma((R,))],
        compiler_params=pltpu.CompilerParams(collective_id=1, has_side_effects=True),
    )(held)


def final_kernel(table, parent, payload, panel, inv_top, inv_low, col_top, col_low, out, high_part, low_part):
    step = pl.program_id(0)
    per, bcols = parent.shape[0], parent.shape[2]
    tile = parent.shape[4]
    blocks = payload.shape[0]
    group = bcols // blocks
    first_active = table[0, 4]
    big_rows = [table[0, 0] + (step * per + p) * table[0, 1] for p in range(per)]
    big_cols = [table[0, 2] + b * table[0, 3] for b in range(bcols)]

    for b in range(bcols):
        for p in range(per):
            place = table[1, step * per + p]
            hit = (place >= 0) & (table[2, b] > 0)
            out[p, 0, b, 0] = parent[p, 0, b, 0]

            @pl.when(hit)
            def _():
                out[p, 0, b, 0] = parent[p, 0, b, 0] + payload[b // group, jnp.maximum(place, 0)]

    @pl.when(big_rows[-1] >= first_active)
    def _():
        stacked = [jnp.concatenate([panel[p, 0, m, 0] for m in range(panel.shape[2])], axis=1) for p in range(per)]
        scaled = dot3(split(jnp.concatenate(stacked, axis=0)), (inv_top[...], inv_low[...]), ((1,), (0,)))
        top, low = split(scaled)
        high_part[...] = top
        low_part[...] = low
        for g in range(blocks):
            @pl.when((big_rows[-1] >= big_cols[g * group]) & (big_cols[g * group + group - 1] >= first_active))
            def _():
                at = pl.ds(g * group * tile, group * tile)
                trailing = dot3((high_part[...], low_part[...]), (col_top[at, :], col_low[at, :]), ((1,), (1,)))
                for q in range(group):
                    b = g * group + q
                    for p in range(per):
                        active = (big_rows[p] >= big_cols[b]) & (big_cols[b] >= first_active)
                        part = trailing[p * tile : (p + 1) * tile, q * tile : (q + 1) * tile]
                        out[p, 0, b, 0] = out[p, 0, b, 0] - jnp.where(active, part, 0.0)


def finish(table, parent, payload, panel, inv, cols):
    rows, _, bcols, _, tile, _ = parent.shape
    per, subs, width, piece = panel.shape[:4]
    whole = lambda a: pl.BlockSpec(a.shape, lambda i, t: (0,) * a.ndim)
    big = pl.BlockSpec((per, 1, bcols, 1, tile, tile), lambda i, t: (i, 0, 0, 0, 0, 0))
    picked = pl.BlockSpec(
        (per, 1, width, 1, tile, tile), lambda i, t: (0, i // piece, 0, i % piece, 0, 0)
    )
    flops = 6 * rows * tile * width * tile * (width + bcols) * tile
    return pl.pallas_call(
        final_kernel,
        grid_spec=pltpu.PrefetchScalarGridSpec(
            num_scalar_prefetch=1,
            grid=(rows // per,),
            in_specs=[big, whole(payload), picked, whole(inv[0]), whole(inv[1]), whole(cols[0]), whole(cols[1])],
            out_specs=big,
            scratch_shapes=[pltpu.VMEM((per * tile, width * tile), bf16)] * 2,
        ),
        out_shape=jax.ShapeDtypeStruct(parent.shape, f32),
        cost_estimate=pl.CostEstimate(flops=flops, bytes_accessed=10 * parent.size, transcendentals=0),
    )(table, parent, payload, panel, *inv, *cols)


def product_kernel(per, tile, table, everyone, out, mine_top, mine_low, their_top, their_low):
    R, T, rank, wide = everyone.shape
    C = out.shape[0]
    width = wide - tile
    for t in range(T):
        top, low = split(everyone[table[1, t // per], t, :, :width])
        mine_top[t * rank : (t + 1) * rank, :] = top
        mine_low[t * rank : (t + 1) * rank, :] = low
    at = 0
    for s in range(T // per):
        for c in range(C):
            src = lax.rem(c + C - table[0, s], C)
            top, low = split(everyone[lax.rem(src, R), s * per + lax.div(src, R), :, :width])
            their_top[c * rank : (c + 1) * rank, :] = top
            their_low[c * rank : (c + 1) * rank, :] = low
        first = s * per * rank
        size = T * rank - first
        mine = (mine_top[first:, :], mine_low[first:, :])
        got = dot3((their_top[...], their_low[...]), mine, ((1,), (1,)))
        out[:, :, at : at + size] = got.reshape(C, rank, size)
        at += size


def products(table, everyone, C, per, tile):
    R, T, rank, wide = everyone.shape
    S = T // per
    total = sum((S - s) * per * rank for s in range(S))
    vmem = pl.BlockSpec(memory_space=pltpu.VMEM)
    width = wide - tile
    return pl.pallas_call(
        lambda *refs: product_kernel(per, tile, *refs),
        in_specs=[pl.BlockSpec(memory_space=pltpu.SMEM), vmem],
        out_specs=vmem,
        out_shape=jax.ShapeDtypeStruct((C, rank, total), f32),
        scratch_shapes=[pltpu.VMEM((T * rank, width), bf16)] * 2 + [pltpu.VMEM((C * rank, width), bf16)] * 2,
        name="products",
    )(table, everyone)


def update_kernel(per, C, table, ranks, weights, bases, *refs):
    moved, out = refs[:-1], refs[-1]
    S, T, tile = out.shape[:3]
    R, _, rank, _ = bases.shape
    depth = lax.broadcasted_iota(jnp.int32, (rank, tile), 0)

    def basis(row, t):
        return split(jnp.where(depth < ranks[t * R + row], bases[row, t], 0.0))

    at = 0
    for s in range(S):
        size = (S - s) * per * rank
        src = table[2, s]
        j = s * C + src
        col_basis = basis(lax.rem(src, R), s * per + lax.div(src, R))
        half = dot3(split(weights[:, at : at + size]), col_basis, ((0,), (0,)))
        at += size
        for t in range(T):
            if t < s * per:
                out[s, t] = jnp.zeros((tile, tile), f32)
                continue
            k = t - s * per
            row = table[1, t // per]
            update = dot3(basis(row, t), split(half[k * rank : (k + 1) * rank]), ((0,), (0,)))
            out[s, t] = jnp.where(t * R + row >= j, moved[s][k] - update, 0.0)


def updates(table, ranks, weights, everyone, moved, C, per):
    R, T, rank, wide = everyone.shape
    S, tile = T // per, moved[0].shape[1]
    smem = pl.BlockSpec(memory_space=pltpu.SMEM)
    whole = lambda a: pl.BlockSpec(a.shape, lambda i: (0,) * a.ndim)
    out = jax.ShapeDtypeStruct((S, T, tile, tile), f32)
    picked = pl.BlockSpec((R, T, rank, tile), lambda i: (0, 0, 0, wide // tile - 1))
    return pl.pallas_call(
        lambda *refs: update_kernel(per, C, *refs),
        grid=(1,),
        in_specs=[smem, smem, whole(weights), picked] + [whole(m) for m in moved],
        out_specs=whole(out),
        out_shape=out,
        name="updates",
    )(table, ranks, weights, everyone, *moved)


def per_device(
    contribution,
    parent_tiles,
    row_basis,
    pivot_basis,
    tile_ranks,
    block_map,
    panel_start,
    pivot_inverse,
):
    R = lax.axis_size("row")
    C = lax.axis_size("col")
    my_row = lax.axis_index("row")
    my_col = lax.axis_index("col")
    T, S = contribution.shape[0], contribution.shape[2]
    tile = contribution.shape[4]
    rows, bcols = parent_tiles.shape[0], parent_tiles.shape[2]
    rank = row_basis.shape[2]
    width = pivot_basis.shape[3]
    per = C // R
    span = rows // S
    shift = [block_map[u * C] - 2 * u * C for u in range(S)]
    src_row = [(my_row - shift[u]) % R for u in range(S)]
    src_col = [(my_col - shift[s]) % C for s in range(S)]

    child = contribution[:, 0, :, 0]
    by_row = [rotate(child[u * per : (u + 1) * per, : u + 1], "row", shift[u] % R) for u in range(S)]

    start = panel_start[0]
    own_b = jnp.minimum((start + (my_col - start) % C) // C, bcols - 1)
    subs = R // PANEL_T
    piece = rows // per // subs
    members = C // PANEL_T
    my_member = my_col // PANEL_T

    def exchange(pieces):
        held = lax.dynamic_index_in_dim(pieces, my_member, axis=0, keepdims=False)
        for k in range(1, members):
            gone = lax.dynamic_index_in_dim(pieces, (my_member + k) % members, axis=0, keepdims=False)
            came = lax.ppermute(gone, "col", [(d, (d + PANEL_T * k) % C) for d in range(C)])
            theirs = (my_col - PANEL_T * k - start) % C < PANEL_T
            held = jnp.where(theirs, came, held)
        return held

    column = lax.dynamic_index_in_dim(parent_tiles[:, 0, :, 0], own_b, axis=1, keepdims=False)
    column = column.reshape(subs, piece, per, tile, tile)
    column = jnp.moveaxis(column, 2, 0).reshape(members, piece, tile, tile)

    factors = jnp.concatenate([pivot_basis[:, 0], row_basis[:, 0]], axis=2)
    everyone = gather_ring(factors, "row")
    everyone, by_row, column = lax.optimization_barrier((everyone, by_row, column))
    held_parent = exchange(column)
    moved = [
        rotate(jnp.concatenate([by_row[u][:, s] for u in range(s, S)], axis=0), "col", shift[s])
        for s in range(S)
    ]
    routes = jnp.stack([jnp.stack(shift), jnp.stack(src_row), jnp.stack(src_col)]).astype(jnp.int32)
    partial = products(routes, everyone, C, per, tile)
    weights = lax.psum_scatter(partial, "col", scatter_dimension=0, tiled=True)[0]
    payload = updates(routes, tile_ranks, weights, everyone, moved, C, per)

    first_row = jnp.stack([(2 * u * C + shift[u] + src_row[u]) // R for u in range(S)])
    a = jnp.arange(rows, dtype=jnp.int32)
    u_of = a // span
    p_of = a - first_row[u_of]
    place = jnp.where((p_of >= 0) & (p_of < per), u_of * per + p_of, -1).astype(jnp.int32)
    target_col = jnp.stack([(2 * s * C + shift[s] + src_col[s]) // C for s in range(S)])
    b = jnp.arange(bcols, dtype=jnp.int32)
    col_hit = (target_col[b // (bcols // S)] == b).astype(jnp.int32)

    child_col = lax.dynamic_index_in_dim(payload, own_b // (bcols // S), axis=0, keepdims=False)
    child_col = child_col.reshape(S, per, tile, tile)
    parity = jnp.arange(per, dtype=jnp.int32)
    holds = (parity[:, None] - first_row[None, :]) % per
    compact = jnp.zeros((per, S, tile, tile), f32)
    for p in range(per):
        compact = compact + jnp.where((holds == p)[:, :, None, None], child_col[None, :, p], 0.0)
    hit = lax.dynamic_index_in_dim(col_hit, own_b, axis=0, keepdims=False) > 0
    compact = jnp.where(hit, compact, 0.0).reshape(members, S // subs, tile, tile)
    held_child = exchange(compact)
    piece_rows = (my_member % subs * piece + jnp.arange(piece, dtype=jnp.int32)) * per + my_member // subs
    landed = jnp.repeat(held_child, span // per, axis=0)
    held = held_parent + jnp.where((place[piece_rows] >= 0)[:, None, None], landed, 0.0)
    panel, cols = gather_panel(held)
    panel = panel.reshape(per, subs, PANEL_T, piece, tile, tile)
    local = lax.dynamic_index_in_dim(panel, my_col // R, axis=0, keepdims=False)
    cols = jnp.where(my_row == my_col % R, local, cols.reshape(local.shape))
    cols = jnp.transpose(cols, (0, 2, 3, 1, 4)).reshape(bcols * tile, PANEL_T * tile)
    inverse = pivot_inverse.reshape(PANEL_T, tile, PANEL_T, tile)
    inverse = jnp.roll(inverse, (start % PANEL_T, start % PANEL_T), axis=(0, 2))
    inverse = inverse.reshape(PANEL_T * tile, PANEL_T * tile)
    scalars = jnp.stack([my_row, R + 0 * my_row, my_col, C + 0 * my_row, start + PANEL_T]).astype(jnp.int32)
    pad = lambda v: jnp.concatenate([v, jnp.zeros((rows - v.shape[0],), jnp.int32)])
    table = jnp.stack([pad(scalars), place, pad(col_hit)])
    return finish(table, parent_tiles, payload, panel, split_outside(inverse), split_outside(cols))


def solution(mesh):
    placed = (
        P(None, "row", None, "col", None, None),
        P(None, "row", None, "col", None, None),
        P(None, "row", None, None),
        P(None, "row", None, "col"),
        P(),
        P(),
        P(),
        P(),
    )
    return jax.shard_map(
        per_device,
        mesh=mesh,
        in_specs=placed,
        out_specs=P(None, "row", None, "col", None, None),
        check_vma=False,
    )
```

```python
import jax
import jax.numpy as jnp
from jax import lax
from jax.experimental import pallas as pl
from jax.experimental.pallas import tpu as pltpu
from jax.sharding import PartitionSpec as P

PANEL_T = 4
f32 = jnp.float32
bf16 = jnp.bfloat16
high = lax.Precision.HIGH


def rotate(x, axis, amount):
    n = lax.axis_size(axis)

    def branch(k):
        pairs = [(d, (d + k) % n) for d in range(n)]
        return (lambda v: v) if k == 0 else (lambda v: lax.ppermute(v, axis, pairs))

    return lax.switch(amount, [branch(k) for k in range(n)], x)


def split(x):
    top = x.astype(bf16)
    return top, (x - top.astype(f32)).astype(bf16)


def split_outside(x):
    top = lax.reduce_precision(x, exponent_bits=8, mantissa_bits=7)
    return top.astype(bf16), (x - top).astype(bf16)


def dot3(a, b, dims):
    (ah, al), (bh, bl) = a, b
    one = lambda p, q: lax.dot_general(p, q, (dims, ((), ())), preferred_element_type=f32)
    return one(ah, bh) + (one(ah, bl) + one(al, bh))


def ring_place(p, n):
    return jnp.where(p < n // 2, 2 * p, 2 * (n - 1 - p) + 1)


def panel_kernel(held, panel, cols, send, recv, own_sem, cross_send, cross_recv, relay_send):
    R, n = lax.axis_size("row"), lax.axis_size("col")
    my_row, me = lax.axis_index("row"), lax.axis_index("col")
    half = held.shape[0] // 2
    pos = jnp.where(me % 2 == 0, me // 2, n - 1 - me // 2)
    right = ring_place((pos + 1) % n, n)
    left = ring_place((pos + n - 1) % n, n)
    root = me % R
    is_root = my_row == root
    mesh_id = pl.DeviceIdType.MESH

    barrier = pltpu.get_barrier_semaphore()
    for side in (left, right):
        pl.semaphore_signal(barrier, inc=1, device_id={"col": side}, device_id_type=mesh_id)
    for k in range(1, R):
        pl.semaphore_signal(barrier, inc=1, device_id={"row": (my_row + k) % R}, device_id_type=mesh_id)
    pl.semaphore_wait(barrier, R + 1)

    chunk = lambda h: pl.ds(h * half, half)
    own = pltpu.make_async_copy(held, panel.at[me], own_sem)
    own.start()

    def block(side, k):
        return ring_place((pos - k + n) % n if side == 0 else (pos + k) % n, n)

    def step(side, k, h):
        d = block(side, k)
        src = held.at[chunk(h)] if k == 0 else panel.at[d, chunk(h)]
        return pltpu.make_async_remote_copy(
            src, panel.at[d, chunk(h)], send.at[side, k, h], recv.at[side, k, h],
            device_id={"col": right if side == 0 else left}, device_id_type=mesh_id)

    def arrival(side, k, h):
        d = block(side, k + 1)
        return pltpu.make_async_remote_copy(
            panel.at[d, chunk(h)], panel.at[d, chunk(h)], send.at[side, k, h], recv.at[side, k, h],
            device_id={"col": right if side == 0 else left}, device_id_type=mesh_id)

    def cross(m, h, o):
        if o == 0:
            to = my_row + 1 - 2 * (my_row % 2)
        else:
            core = my_row % 2 if h == 0 else 1 - my_row % 2
            to = (my_row // 2 + o) % (R // 2) * 2 + core
        src = panel.at[me // R * R + m, chunk(h)]
        return pltpu.make_async_remote_copy(
            src, cols.at[m, chunk(h)], cross_send.at[m, h, o], cross_recv.at[m, h],
            device_id={"row": to}, device_id_type=mesh_id)

    def forward(d, h, ready=True):
        @pl.when(is_root & (d // R == me // R))
        def _():
            for o in range(1, R // 2):
                cross(d % R, h, o).start()
            cross(d % R, h, 0).start()

    last = n // 2 - 1
    used = [(side, k, h) for k in range(n // 2) for h in range(2) for side in range(2) if k < last or h == side]
    for side, k, h in used:
        if k > 0:
            arrival(side, k - 1, h).wait_recv()
        step(side, k, h).start()
        if k > 0:
            forward(block(side, k), h)
        elif side == 0 and h == 1:
            own.wait()
            forward(me, 0)
            forward(me, 1)
    for side in range(2):
        arrival(side, last - 1, 1 - side).wait_recv()
        forward(block(side, last), 1 - side)
    for side in range(2):
        arrival(side, last, side).wait_recv()
        forward(block(side, last + 1), side)

    @pl.when(is_root)
    def _():
        for m in range(R):
            for h in range(2):
                for o in range(R // 2):
                    cross(m, h, o).wait_send()

    def relay(m, h):
        to = my_row + 1 - 2 * (my_row % 2)
        return pltpu.make_async_remote_copy(
            cols.at[m, chunk(h)], cols.at[m, chunk(h)], relay_send.at[m], cross_recv.at[m, h],
            device_id={"row": to}, device_id_type=mesh_id)

    @pl.when(~is_root & (my_row // 2 == root // 2))
    def _():
        for m in range(R):
            for h in range(2):
                relay(m, h).wait_recv()

    for mine in range(2):
        @pl.when((my_row // 2 != root // 2) & ((my_row + root) % 2 == mine))
        def _():
            for m in range(R):
                relay(m, mine).wait_recv()
                relay(m, mine).start()
            for m in range(R):
                relay(m, 1 - mine).wait_recv()
            for m in range(R):
                relay(m, mine).wait_send()

    for side, k, h in used:
        step(side, k, h).wait_send()


def gather_panel(held):
    R, n = lax.axis_size("row"), lax.axis_size("col")
    dma = pltpu.SemaphoreType.DMA
    anywhere = pl.BlockSpec(memory_space=pl.ANY)
    return pl.pallas_call(
        panel_kernel,
        in_specs=[pl.BlockSpec(memory_space=pltpu.VMEM)],
        out_specs=(anywhere, anywhere),
        out_shape=(jax.ShapeDtypeStruct((n,) + held.shape, f32), jax.ShapeDtypeStruct((R,) + held.shape, f32)),
        scratch_shapes=[dma((2, n // 2, 2)), dma((2, n // 2, 2)), dma, dma((R, 2, R // 2)), dma((R, 2)), dma((R,))],
        compiler_params=pltpu.CompilerParams(collective_id=1, has_side_effects=True),
    )(held)


def final_kernel(table, parent, payload, panel, inv_top, inv_low, col_top, col_low, out, high_part, low_part):
    step = pl.program_id(0)
    per, bcols = parent.shape[0], parent.shape[2]
    tile = parent.shape[4]
    blocks = payload.shape[0]
    group = bcols // blocks
    first_active = table[0, 4]
    big_rows = [table[0, 0] + (step * per + p) * table[0, 1] for p in range(per)]
    big_cols = [table[0, 2] + b * table[0, 3] for b in range(bcols)]

    for b in range(bcols):
        for p in range(per):
            place = table[1, step * per + p]
            hit = (place >= 0) & (table[2, b] > 0)
            out[p, 0, b, 0] = parent[p, 0, b, 0]

            @pl.when(hit)
            def _():
                out[p, 0, b, 0] = parent[p, 0, b, 0] + payload[b // group, jnp.maximum(place, 0)]

    @pl.when(big_rows[-1] >= first_active)
    def _():
        stacked = [jnp.concatenate([panel[p, 0, m, 0] for m in range(panel.shape[2])], axis=1) for p in range(per)]
        scaled = dot3(split(jnp.concatenate(stacked, axis=0)), (inv_top[...], inv_low[...]), ((1,), (0,)))
        top, low = split(scaled)
        high_part[...] = top
        low_part[...] = low
        for g in range(blocks):
            @pl.when((big_rows[-1] >= big_cols[g * group]) & (big_cols[g * group + group - 1] >= first_active))
            def _():
                at = pl.ds(g * group * tile, group * tile)
                trailing = dot3((high_part[...], low_part[...]), (col_top[at, :], col_low[at, :]), ((1,), (1,)))
                for q in range(group):
                    b = g * group + q
                    for p in range(per):
                        active = (big_rows[p] >= big_cols[b]) & (big_cols[b] >= first_active)
                        part = trailing[p * tile : (p + 1) * tile, q * tile : (q + 1) * tile]
                        out[p, 0, b, 0] = out[p, 0, b, 0] - jnp.where(active, part, 0.0)


def finish(table, parent, payload, panel, inv, cols):
    rows, _, bcols, _, tile, _ = parent.shape
    per, subs, width, piece = panel.shape[:4]
    whole = lambda a: pl.BlockSpec(a.shape, lambda i, t: (0,) * a.ndim)
    big = pl.BlockSpec((per, 1, bcols, 1, tile, tile), lambda i, t: (i, 0, 0, 0, 0, 0))
    picked = pl.BlockSpec(
        (per, 1, width, 1, tile, tile), lambda i, t: (0, i // piece, 0, i % piece, 0, 0)
    )
    flops = 6 * rows * tile * width * tile * (width + bcols) * tile
    return pl.pallas_call(
        final_kernel,
        grid_spec=pltpu.PrefetchScalarGridSpec(
            num_scalar_prefetch=1,
            grid=(rows // per,),
            in_specs=[big, whole(payload), picked, whole(inv[0]), whole(inv[1]), whole(cols[0]), whole(cols[1])],
            out_specs=big,
            scratch_shapes=[pltpu.VMEM((per * tile, width * tile), bf16)] * 2,
        ),
        out_shape=jax.ShapeDtypeStruct(parent.shape, f32),
        cost_estimate=pl.CostEstimate(flops=flops, bytes_accessed=10 * parent.size, transcendentals=0),
    )(table, parent, payload, panel, *inv, *cols)


def greet(targets):
    barrier = pltpu.get_barrier_semaphore()
    for target in targets:
        pl.semaphore_signal(barrier, inc=1, device_id=target, device_id_type=pl.DeviceIdType.MESH)
    pl.semaphore_wait(barrier, len(targets))


def row_gather_kernel(mine, everyone, own_sem, send, recv, relay_send):
    R = lax.axis_size("row")
    me = lax.axis_index("row")
    pairs = R // 2
    other = me + 1 - 2 * (me % 2)
    greet([{"row": (me + k) % R} for k in range(1, R)])
    own = pltpu.make_async_copy(mine, everyone.at[me], own_sem)
    own.start()

    def direct(o):
        to = other if o == 0 else (me // 2 + o) % pairs * 2 + me % 2
        return pltpu.make_async_remote_copy(
            mine, everyone.at[me], send.at[o], recv.at[o, 0], device_id={"row": to},
            device_id_type=pl.DeviceIdType.MESH)

    def source(o):
        return (me // 2 - o + pairs) % pairs * 2 + me % 2

    def relay(o, d):
        return pltpu.make_async_remote_copy(
            everyone.at[d], everyone.at[d], relay_send.at[o], recv.at[o, 1], device_id={"row": other},
            device_id_type=pl.DeviceIdType.MESH)

    for o in list(range(1, pairs)) + [0]:
        direct(o).start()
    for o in range(1, pairs):
        direct(o).wait_recv()
        relay(o, source(o)).start()
    direct(0).wait_recv()
    for o in range(1, pairs):
        relay(o, source(o)).wait_recv()
        relay(o, source(o)).wait_send()
    for o in range(pairs):
        direct(o).wait_send()
    own.wait()


def row_gather(mine):
    R = lax.axis_size("row")
    dma = pltpu.SemaphoreType.DMA
    return pl.pallas_call(
        row_gather_kernel,
        in_specs=[pl.BlockSpec(memory_space=pltpu.VMEM)],
        out_specs=pl.BlockSpec(memory_space=pltpu.VMEM),
        out_shape=jax.ShapeDtypeStruct((R,) + mine.shape, f32),
        scratch_shapes=[dma, dma((R // 2,)), dma((R // 2, 2)), dma((R // 2,))],
        compiler_params=pltpu.CompilerParams(collective_id=2, has_side_effects=True),
        name="row_gather",
    )(mine)


def ring_sum_kernel(partial, out, slots, send, recv):
    n = lax.axis_size("col")
    me = lax.axis_index("col")
    chunk = partial.shape[1] // 4
    pos = jnp.where(me % 2 == 0, me // 2, n - 1 - me // 2)
    right = ring_place((pos + 1) % n, n)
    left = ring_place((pos + n - 1) % n, n)
    greet([{"col": left}, {"col": right}])
    rows = lambda side, h: pl.ds((2 * side + h) * chunk, chunk)

    def part(side, k, h):
        q = (pos - 1 - k + n) % n if side == 0 else (pos + 1 + k) % n
        return partial.at[ring_place(q, n), rows(side, h)]

    def hop(side, k, h):
        src = part(side, 0, h) if k == 0 else slots.at[side, k - 1, h]
        return pltpu.make_async_remote_copy(
            src, slots.at[side, k, h], send.at[side, k, h], recv.at[side, k, h],
            device_id={"col": right if side == 0 else left}, device_id_type=pl.DeviceIdType.MESH)

    every = [(k, h, side) for k in range(n - 1) for h in range(2) for side in range(2)]
    for k, h, side in every:
        if k > 0:
            hop(side, k - 1, h).wait_recv()
            slots[side, k - 1, h] = slots[side, k - 1, h] + part(side, k, h)[...]
        hop(side, k, h).start()
    for h in range(2):
        for side in range(2):
            hop(side, n - 2, h).wait_recv()
            out[rows(side, h), :] = slots[side, n - 2, h] + partial[me, rows(side, h), :]
    for k, h, side in every:
        hop(side, k, h).wait_send()


def ring_sum(partial):
    n, rank, total = partial.shape
    dma = pltpu.SemaphoreType.DMA
    vmem = pl.BlockSpec(memory_space=pltpu.VMEM)
    return pl.pallas_call(
        ring_sum_kernel,
        in_specs=[vmem],
        out_specs=vmem,
        out_shape=jax.ShapeDtypeStruct((rank, total), f32),
        scratch_shapes=[pltpu.VMEM((2, n - 1, 2, rank // 4, total), f32), dma((2, n - 1, 2)), dma((2, n - 1, 2))],
        compiler_params=pltpu.CompilerParams(collective_id=3, has_side_effects=True),
        name="ring_sum",
    )(partial)


def product_kernel(per, tile, table, everyone, out, mine_top, mine_low, their_top, their_low):
    R, T, rank, wide = everyone.shape
    C = out.shape[0]
    width = wide - tile
    for t in range(T):
        top, low = split(everyone[table[1, t // per], t, :, :width])
        mine_top[t * rank : (t + 1) * rank, :] = top
        mine_low[t * rank : (t + 1) * rank, :] = low
    at = 0
    for s in range(T // per):
        for c in range(C):
            src = lax.rem(c + C - table[0, s], C)
            top, low = split(everyone[lax.rem(src, R), s * per + lax.div(src, R), :, :width])
            their_top[c * rank : (c + 1) * rank, :] = top
            their_low[c * rank : (c + 1) * rank, :] = low
        first = s * per * rank
        size = T * rank - first
        mine = (mine_top[first:, :], mine_low[first:, :])
        got = dot3((their_top[...], their_low[...]), mine, ((1,), (1,)))
        out[:, :, at : at + size] = got.reshape(C, rank, size)
        at += size


def products(table, everyone, C, per, tile):
    R, T, rank, wide = everyone.shape
    S = T // per
    total = sum((S - s) * per * rank for s in range(S))
    vmem = pl.BlockSpec(memory_space=pltpu.VMEM)
    width = wide - tile
    return pl.pallas_call(
        lambda *refs: product_kernel(per, tile, *refs),
        in_specs=[pl.BlockSpec(memory_space=pltpu.SMEM), vmem],
        out_specs=vmem,
        out_shape=jax.ShapeDtypeStruct((C, rank, total), f32),
        scratch_shapes=[pltpu.VMEM((T * rank, width), bf16)] * 2 + [pltpu.VMEM((C * rank, width), bf16)] * 2,
        name="products",
    )(table, everyone)


def update_kernel(per, C, table, ranks, weights, bases, *refs):
    moved, out = refs[:-1], refs[-1]
    S, T, tile = out.shape[:3]
    R, _, rank, _ = bases.shape
    depth = lax.broadcasted_iota(jnp.int32, (rank, tile), 0)

    def basis(row, t):
        return split(jnp.where(depth < ranks[t * R + row], bases[row, t], 0.0))

    at = 0
    for s in range(S):
        size = (S - s) * per * rank
        src = table[2, s]
        j = s * C + src
        col_basis = basis(lax.rem(src, R), s * per + lax.div(src, R))
        half = dot3(split(weights[:, at : at + size]), col_basis, ((0,), (0,)))
        at += size
        for t in range(T):
            if t < s * per:
                out[s, t] = jnp.zeros((tile, tile), f32)
                continue
            k = t - s * per
            row = table[1, t // per]
            update = dot3(basis(row, t), split(half[k * rank : (k + 1) * rank]), ((0,), (0,)))
            out[s, t] = jnp.where(t * R + row >= j, moved[s][k] - update, 0.0)


def updates(table, ranks, weights, everyone, moved, C, per):
    R, T, rank, wide = everyone.shape
    S, tile = T // per, moved[0].shape[1]
    smem = pl.BlockSpec(memory_space=pltpu.SMEM)
    whole = lambda a: pl.BlockSpec(a.shape, lambda i: (0,) * a.ndim)
    out = jax.ShapeDtypeStruct((S, T, tile, tile), f32)
    picked = pl.BlockSpec((R, T, rank, tile), lambda i: (0, 0, 0, wide // tile - 1))
    return pl.pallas_call(
        lambda *refs: update_kernel(per, C, *refs),
        grid=(1,),
        in_specs=[smem, smem, whole(weights), picked] + [whole(m) for m in moved],
        out_specs=whole(out),
        out_shape=out,
        name="updates",
    )(table, ranks, weights, everyone, *moved)


def per_device(
    contribution,
    parent_tiles,
    row_basis,
    pivot_basis,
    tile_ranks,
    block_map,
    panel_start,
    pivot_inverse,
):
    R = lax.axis_size("row")
    C = lax.axis_size("col")
    my_row = lax.axis_index("row")
    my_col = lax.axis_index("col")
    T, S = contribution.shape[0], contribution.shape[2]
    tile = contribution.shape[4]
    rows, bcols = parent_tiles.shape[0], parent_tiles.shape[2]
    rank = row_basis.shape[2]
    width = pivot_basis.shape[3]
    per = C // R
    span = rows // S
    block = jnp.arange(S, dtype=jnp.int32)
    shift = block_map.reshape(S, C)[:, 0] - 2 * C * block
    src_row = lax.rem(my_row + C * R - shift, jnp.full_like(shift, R))
    src_col = lax.rem(my_col + C - shift, jnp.full_like(shift, C))
    row_shift = lax.rem(shift, jnp.full_like(shift, R))

    child = contribution[:, 0, :, 0]
    by_row = [rotate(child[u * per : (u + 1) * per, : u + 1], "row", row_shift[u]) for u in range(S)]

    start = panel_start[0]
    own_b = jnp.minimum((start + (my_col - start) % C) // C, bcols - 1)
    subs = R // PANEL_T
    piece = rows // per // subs
    members = C // PANEL_T
    my_member = my_col // PANEL_T

    def exchange(pieces):
        held = lax.dynamic_index_in_dim(pieces, my_member, axis=0, keepdims=False)
        for k in range(1, members):
            gone = lax.dynamic_index_in_dim(pieces, (my_member + k) % members, axis=0, keepdims=False)
            came = lax.ppermute(gone, "col", [(d, (d + PANEL_T * k) % C) for d in range(C)])
            theirs = (my_col - PANEL_T * k - start) % C < PANEL_T
            held = jnp.where(theirs, came, held)
        return held

    column = lax.dynamic_index_in_dim(parent_tiles[:, 0, :, 0], own_b, axis=1, keepdims=False)
    column = column.reshape(subs, piece, per, tile, tile)
    column = jnp.moveaxis(column, 2, 0).reshape(members, piece, tile, tile)

    factors = jnp.concatenate([pivot_basis[:, 0], row_basis[:, 0]], axis=2)
    column, factors = lax.optimization_barrier((column, factors))
    held_parent = exchange(column)
    everyone = row_gather(factors)
    everyone, by_row, held_parent = lax.optimization_barrier((everyone, by_row, held_parent))
    moved = [
        rotate(jnp.concatenate([by_row[u][:, s] for u in range(s, S)], axis=0), "col", shift[s])
        for s in range(S)
    ]
    routes = jnp.stack([shift, src_row, src_col])
    partial = products(routes, everyone, C, per, tile)
    weights = ring_sum(partial)
    payload = updates(routes, tile_ranks, weights, everyone, moved, C, per)

    first_row = lax.div(2 * C * block + shift + src_row, jnp.full_like(shift, R))
    a = jnp.arange(rows, dtype=jnp.int32)
    p_of = a - jnp.repeat(first_row, span)
    u_of = a // span
    place = jnp.where((p_of >= 0) & (p_of < per), u_of * per + p_of, -1).astype(jnp.int32)
    target_col = lax.div(2 * C * block + shift + src_col, jnp.full_like(shift, C))
    b = jnp.arange(bcols, dtype=jnp.int32)
    col_hit = (jnp.repeat(target_col, bcols // S) == b).astype(jnp.int32)

    child_col = lax.dynamic_index_in_dim(payload, own_b // (bcols // S), axis=0, keepdims=False)
    child_col = child_col.reshape(S, per, tile, tile)
    parity = jnp.arange(per, dtype=jnp.int32)
    holds = (parity[:, None] - first_row[None, :]) % per
    compact = jnp.zeros((per, S, tile, tile), f32)
    for p in range(per):
        compact = compact + jnp.where((holds == p)[:, :, None, None], child_col[None, :, p], 0.0)
    hit = lax.dynamic_index_in_dim(col_hit, own_b, axis=0, keepdims=False) > 0
    compact = jnp.where(hit, compact, 0.0).reshape(members, S // subs, tile, tile)
    held_child = exchange(compact)
    piece_rows = (my_member % subs * piece + jnp.arange(piece, dtype=jnp.int32)) * per + my_member // subs
    landed = jnp.repeat(held_child, span // per, axis=0)
    held = held_parent + jnp.where((place[piece_rows] >= 0)[:, None, None], landed, 0.0)
    panel, cols = gather_panel(held)
    panel = panel.reshape(per, subs, PANEL_T, piece, tile, tile)
    local = lax.dynamic_index_in_dim(panel, my_col // R, axis=0, keepdims=False)
    cols = jnp.where(my_row == my_col % R, local, cols.reshape(local.shape))
    cols = jnp.transpose(cols, (0, 2, 3, 1, 4)).reshape(bcols * tile, PANEL_T * tile)
    inverse = pivot_inverse.reshape(PANEL_T, tile, PANEL_T, tile)
    inverse = jnp.roll(inverse, (start % PANEL_T, start % PANEL_T), axis=(0, 2))
    inverse = inverse.reshape(PANEL_T * tile, PANEL_T * tile)
    scalars = jnp.stack([my_row, R + 0 * my_row, my_col, C + 0 * my_row, start + PANEL_T]).astype(jnp.int32)
    pad = lambda v: jnp.concatenate([v, jnp.zeros((rows - v.shape[0],), jnp.int32)])
    table = jnp.stack([pad(scalars), place, pad(col_hit)])
    return finish(table, parent_tiles, payload, panel, split_outside(inverse), split_outside(cols))


def solution(mesh):
    placed = (
        P(None, "row", None, "col", None, None),
        P(None, "row", None, "col", None, None),
        P(None, "row", None, None),
        P(None, "row", None, "col"),
        P(),
        P(),
        P(),
        P(),
    )
    return jax.shard_map(
        per_device,
        mesh=mesh,
        in_specs=placed,
        out_specs=P(None, "row", None, "col", None, None),
        check_vma=False,
    )
```

```python
import jax
import jax.numpy as jnp
from jax import lax
from jax.experimental import pallas as pl
from jax.experimental.pallas import tpu as pltpu
from jax.sharding import PartitionSpec as P

PANEL_T = 4
f32 = jnp.float32
bf16 = jnp.bfloat16
high = lax.Precision.HIGH


def rotate(x, axis, amount):
    n = lax.axis_size(axis)

    def branch(k):
        pairs = [(d, (d + k) % n) for d in range(n)]
        return (lambda v: v) if k == 0 else (lambda v: lax.ppermute(v, axis, pairs))

    return lax.switch(amount, [branch(k) for k in range(n)], x)


def split(x):
    top = x.astype(bf16)
    return top, (x - top.astype(f32)).astype(bf16)


def split_outside(x):
    top = lax.reduce_precision(x, exponent_bits=8, mantissa_bits=7)
    return top.astype(bf16), (x - top).astype(bf16)


def dot3(a, b, dims):
    (ah, al), (bh, bl) = a, b
    one = lambda p, q: lax.dot_general(p, q, (dims, ((), ())), preferred_element_type=f32)
    return one(ah, bh) + (one(ah, bl) + one(al, bh))


def ring_place(p, n):
    return jnp.where(p < n // 2, 2 * p, 2 * (n - 1 - p) + 1)


def panel_kernel(held, panel, cols, send, recv, own_sem, cross_send, cross_recv, relay_send):
    R, n = lax.axis_size("row"), lax.axis_size("col")
    my_row, me = lax.axis_index("row"), lax.axis_index("col")
    half = held.shape[0] // 2
    pos = jnp.where(me % 2 == 0, me // 2, n - 1 - me // 2)
    right = ring_place((pos + 1) % n, n)
    left = ring_place((pos + n - 1) % n, n)
    root = me % R
    is_root = my_row == root
    mesh_id = pl.DeviceIdType.MESH

    barrier = pltpu.get_barrier_semaphore()
    for side in (left, right):
        pl.semaphore_signal(barrier, inc=1, device_id={"col": side}, device_id_type=mesh_id)
    for k in range(1, R):
        pl.semaphore_signal(barrier, inc=1, device_id={"row": (my_row + k) % R}, device_id_type=mesh_id)
    pl.semaphore_wait(barrier, R + 1)

    chunk = lambda h: pl.ds(h * half, half)
    own = pltpu.make_async_copy(held, panel.at[me], own_sem)
    own.start()

    def block(side, k):
        return ring_place((pos - k + n) % n if side == 0 else (pos + k) % n, n)

    def step(side, k, h):
        d = block(side, k)
        src = held.at[chunk(h)] if k == 0 else panel.at[d, chunk(h)]
        return pltpu.make_async_remote_copy(
            src, panel.at[d, chunk(h)], send.at[side, k, h], recv.at[side, k, h],
            device_id={"col": right if side == 0 else left}, device_id_type=mesh_id)

    def arrival(side, k, h):
        d = block(side, k + 1)
        return pltpu.make_async_remote_copy(
            panel.at[d, chunk(h)], panel.at[d, chunk(h)], send.at[side, k, h], recv.at[side, k, h],
            device_id={"col": right if side == 0 else left}, device_id_type=mesh_id)

    def cross(m, h, o):
        if o == 0:
            to = my_row + 1 - 2 * (my_row % 2)
        else:
            core = my_row % 2 if h == 0 else 1 - my_row % 2
            to = (my_row // 2 + o) % (R // 2) * 2 + core
        src = panel.at[me // R * R + m, chunk(h)]
        return pltpu.make_async_remote_copy(
            src, cols.at[m, chunk(h)], cross_send.at[m, h, o], cross_recv.at[m, h],
            device_id={"row": to}, device_id_type=mesh_id)

    def forward(d, h, ready=True):
        @pl.when(is_root & (d // R == me // R))
        def _():
            for o in range(1, R // 2):
                cross(d % R, h, o).start()
            cross(d % R, h, 0).start()

    last = n // 2 - 1
    used = [(side, k, h) for k in range(n // 2) for h in range(2) for side in range(2) if k < last or h == side]
    for side, k, h in used:
        if k > 0:
            arrival(side, k - 1, h).wait_recv()
        step(side, k, h).start()
        if k > 0:
            forward(block(side, k), h)
        elif side == 0 and h == 1:
            own.wait()
            forward(me, 0)
            forward(me, 1)
    for side in range(2):
        arrival(side, last - 1, 1 - side).wait_recv()
        forward(block(side, last), 1 - side)
    for side in range(2):
        arrival(side, last, side).wait_recv()
        forward(block(side, last + 1), side)

    @pl.when(is_root)
    def _():
        for m in range(R):
            for h in range(2):
                for o in range(R // 2):
                    cross(m, h, o).wait_send()

    def relay(m, h):
        to = my_row + 1 - 2 * (my_row % 2)
        return pltpu.make_async_remote_copy(
            cols.at[m, chunk(h)], cols.at[m, chunk(h)], relay_send.at[m], cross_recv.at[m, h],
            device_id={"row": to}, device_id_type=mesh_id)

    @pl.when(~is_root & (my_row // 2 == root // 2))
    def _():
        for m in range(R):
            for h in range(2):
                relay(m, h).wait_recv()

    for mine in range(2):
        @pl.when((my_row // 2 != root // 2) & ((my_row + root) % 2 == mine))
        def _():
            for m in range(R):
                relay(m, mine).wait_recv()
                relay(m, mine).start()
            for m in range(R):
                relay(m, 1 - mine).wait_recv()
            for m in range(R):
                relay(m, mine).wait_send()

    for side, k, h in used:
        step(side, k, h).wait_send()


def gather_panel(held):
    R, n = lax.axis_size("row"), lax.axis_size("col")
    dma = pltpu.SemaphoreType.DMA
    anywhere = pl.BlockSpec(memory_space=pl.ANY)
    return pl.pallas_call(
        panel_kernel,
        in_specs=[pl.BlockSpec(memory_space=pltpu.VMEM)],
        out_specs=(anywhere, anywhere),
        out_shape=(jax.ShapeDtypeStruct((n,) + held.shape, f32), jax.ShapeDtypeStruct((R,) + held.shape, f32)),
        scratch_shapes=[dma((2, n // 2, 2)), dma((2, n // 2, 2)), dma, dma((R, 2, R // 2)), dma((R, 2)), dma((R,))],
        compiler_params=pltpu.CompilerParams(collective_id=1, has_side_effects=True),
    )(held)


def final_kernel(table, parent, payload, panel, inv_top, inv_low, col_top, col_low, out, high_part, low_part):
    step = pl.program_id(0)
    per, bcols = parent.shape[0], parent.shape[2]
    tile = parent.shape[4]
    blocks = payload.shape[0]
    group = bcols // blocks
    first_active = table[0, 4]
    big_rows = [table[0, 0] + (step * per + p) * table[0, 1] for p in range(per)]
    big_cols = [table[0, 2] + b * table[0, 3] for b in range(bcols)]

    for b in range(bcols):
        for p in range(per):
            place = table[1, step * per + p]
            hit = (place >= 0) & (table[2, b] > 0)
            out[p, 0, b, 0] = parent[p, 0, b, 0]

            @pl.when(hit)
            def _():
                out[p, 0, b, 0] = parent[p, 0, b, 0] + payload[b // group, jnp.maximum(place, 0)]

    @pl.when(big_rows[-1] >= first_active)
    def _():
        stacked = [jnp.concatenate([panel[p, 0, m, 0] for m in range(panel.shape[2])], axis=1) for p in range(per)]
        scaled = dot3(split(jnp.concatenate(stacked, axis=0)), (inv_top[...], inv_low[...]), ((1,), (0,)))
        top, low = split(scaled)
        high_part[...] = top
        low_part[...] = low
        for g in range(blocks):
            @pl.when((big_rows[-1] >= big_cols[g * group]) & (big_cols[g * group + group - 1] >= first_active))
            def _():
                at = pl.ds(g * group * tile, group * tile)
                trailing = dot3((high_part[...], low_part[...]), (col_top[at, :], col_low[at, :]), ((1,), (1,)))
                for q in range(group):
                    b = g * group + q
                    for p in range(per):
                        active = (big_rows[p] >= big_cols[b]) & (big_cols[b] >= first_active)
                        part = trailing[p * tile : (p + 1) * tile, q * tile : (q + 1) * tile]
                        out[p, 0, b, 0] = out[p, 0, b, 0] - jnp.where(active, part, 0.0)


def finish(table, parent, payload, panel, inv, cols):
    rows, _, bcols, _, tile, _ = parent.shape
    per, subs, width, piece = panel.shape[:4]
    whole = lambda a: pl.BlockSpec(a.shape, lambda i, t: (0,) * a.ndim)
    big = pl.BlockSpec((per, 1, bcols, 1, tile, tile), lambda i, t: (i, 0, 0, 0, 0, 0))
    picked = pl.BlockSpec(
        (per, 1, width, 1, tile, tile), lambda i, t: (0, i // piece, 0, i % piece, 0, 0)
    )
    flops = 6 * rows * tile * width * tile * (width + bcols) * tile
    return pl.pallas_call(
        final_kernel,
        grid_spec=pltpu.PrefetchScalarGridSpec(
            num_scalar_prefetch=1,
            grid=(rows // per,),
            in_specs=[big, whole(payload), picked, whole(inv[0]), whole(inv[1]), whole(cols[0]), whole(cols[1])],
            out_specs=big,
            scratch_shapes=[pltpu.VMEM((per * tile, width * tile), bf16)] * 2,
        ),
        out_shape=jax.ShapeDtypeStruct(parent.shape, f32),
        cost_estimate=pl.CostEstimate(flops=flops, bytes_accessed=10 * parent.size, transcendentals=0),
    )(table, parent, payload, panel, *inv, *cols)


def greet(targets):
    barrier = pltpu.get_barrier_semaphore()
    for target in targets:
        pl.semaphore_signal(barrier, inc=1, device_id=target, device_id_type=pl.DeviceIdType.MESH)
    pl.semaphore_wait(barrier, len(targets))


def row_gather_kernel(mine, everyone, own_sem, send, recv, relay_send):
    R = lax.axis_size("row")
    me = lax.axis_index("row")
    pairs = R // 2
    other = me + 1 - 2 * (me % 2)
    greet([{"row": (me + k) % R} for k in range(1, R)])
    own = pltpu.make_async_copy(mine, everyone.at[me], own_sem)
    own.start()

    parts = 4
    size = mine.shape[0] // parts

    def direct(o, h):
        to = other if o == 0 else (me // 2 + o) % pairs * 2 + me % 2
        at = pl.ds(h * size, size)
        return pltpu.make_async_remote_copy(
            mine.at[at], everyone.at[me, at], send.at[o, h], recv.at[o, 0, h], device_id={"row": to},
            device_id_type=pl.DeviceIdType.MESH)

    def relay(o, h):
        d = (me // 2 - o + pairs) % pairs * 2 + me % 2
        at = pl.ds(h * size, size)
        return pltpu.make_async_remote_copy(
            everyone.at[d, at], everyone.at[d, at], relay_send.at[o, h], recv.at[o, 1, h], device_id={"row": other},
            device_id_type=pl.DeviceIdType.MESH)

    away = [(o, h) for h in range(parts) for o in range(1, pairs)]
    near = [(0, h) for h in range(parts)]
    for o, h in away + near:
        direct(o, h).start()
    for o, h in away:
        direct(o, h).wait_recv()
        relay(o, h).start()
    for o, h in near:
        direct(o, h).wait_recv()
    for o, h in away:
        relay(o, h).wait_recv()
        relay(o, h).wait_send()
    for o, h in away + near:
        direct(o, h).wait_send()
    own.wait()


def row_gather(mine):
    R = lax.axis_size("row")
    dma = pltpu.SemaphoreType.DMA
    return pl.pallas_call(
        row_gather_kernel,
        in_specs=[pl.BlockSpec(memory_space=pltpu.VMEM)],
        out_specs=pl.BlockSpec(memory_space=pltpu.VMEM),
        out_shape=jax.ShapeDtypeStruct((R,) + mine.shape, f32),
        scratch_shapes=[dma, dma((R // 2, 4)), dma((R // 2, 2, 4)), dma((R // 2, 4))],
        compiler_params=pltpu.CompilerParams(collective_id=2, has_side_effects=True),
        name="row_gather",
    )(mine)


def ring_sum_kernel(partial, out, slots, send, recv):
    n = lax.axis_size("col")
    me = lax.axis_index("col")
    chunk = partial.shape[1] // 4
    pos = jnp.where(me % 2 == 0, me // 2, n - 1 - me // 2)
    right = ring_place((pos + 1) % n, n)
    left = ring_place((pos + n - 1) % n, n)
    greet([{"col": left}, {"col": right}])
    rows = lambda side, h: pl.ds((2 * side + h) * chunk, chunk)

    def part(side, k, h):
        q = (pos - 1 - k + n) % n if side == 0 else (pos + 1 + k) % n
        return partial.at[ring_place(q, n), rows(side, h)]

    def hop(side, k, h):
        src = part(side, 0, h) if k == 0 else slots.at[side, k - 1, h]
        return pltpu.make_async_remote_copy(
            src, slots.at[side, k, h], send.at[side, k, h], recv.at[side, k, h],
            device_id={"col": right if side == 0 else left}, device_id_type=pl.DeviceIdType.MESH)

    every = [(k, h, side) for k in range(n - 1) for h in range(2) for side in range(2)]
    for k, h, side in every:
        if k > 0:
            hop(side, k - 1, h).wait_recv()
            slots[side, k - 1, h] = slots[side, k - 1, h] + part(side, k, h)[...]
        hop(side, k, h).start()
    for h in range(2):
        for side in range(2):
            hop(side, n - 2, h).wait_recv()
            out[rows(side, h), :] = slots[side, n - 2, h] + partial[me, rows(side, h), :]
    for k, h, side in every:
        hop(side, k, h).wait_send()


def ring_sum(partial):
    n, rank, total = partial.shape
    dma = pltpu.SemaphoreType.DMA
    vmem = pl.BlockSpec(memory_space=pltpu.VMEM)
    return pl.pallas_call(
        ring_sum_kernel,
        in_specs=[vmem],
        out_specs=vmem,
        out_shape=jax.ShapeDtypeStruct((rank, total), f32),
        scratch_shapes=[pltpu.VMEM((2, n - 1, 2, rank // 4, total), f32), dma((2, n - 1, 2)), dma((2, n - 1, 2))],
        compiler_params=pltpu.CompilerParams(collective_id=3, has_side_effects=True),
        name="ring_sum",
    )(partial)


def product_kernel(per, tile, table, everyone, out, mine_top, mine_low, their_top, their_low):
    R, T, rank, wide = everyone.shape
    C = out.shape[0]
    width = wide - tile
    for t in range(T):
        top, low = split(everyone[table[1, t // per], t, :, :width])
        mine_top[t * rank : (t + 1) * rank, :] = top
        mine_low[t * rank : (t + 1) * rank, :] = low
    at = 0
    for s in range(T // per):
        for c in range(C):
            src = lax.rem(c + C - table[0, s], C)
            top, low = split(everyone[lax.rem(src, R), s * per + lax.div(src, R), :, :width])
            their_top[c * rank : (c + 1) * rank, :] = top
            their_low[c * rank : (c + 1) * rank, :] = low
        first = s * per * rank
        size = T * rank - first
        mine = (mine_top[first:, :], mine_low[first:, :])
        got = dot3((their_top[...], their_low[...]), mine, ((1,), (1,)))
        out[:, :, at : at + size] = got.reshape(C, rank, size)
        at += size


def products(table, everyone, C, per, tile):
    R, T, rank, wide = everyone.shape
    S = T // per
    total = sum((S - s) * per * rank for s in range(S))
    vmem = pl.BlockSpec(memory_space=pltpu.VMEM)
    width = wide - tile
    return pl.pallas_call(
        lambda *refs: product_kernel(per, tile, *refs),
        in_specs=[pl.BlockSpec(memory_space=pltpu.SMEM), vmem],
        out_specs=vmem,
        out_shape=jax.ShapeDtypeStruct((C, rank, total), f32),
        scratch_shapes=[pltpu.VMEM((T * rank, width), bf16)] * 2 + [pltpu.VMEM((C * rank, width), bf16)] * 2,
        name="products",
    )(table, everyone)


def update_kernel(per, C, table, ranks, weights, bases, *refs):
    moved, out = refs[:-1], refs[-1]
    S, T, tile = out.shape[:3]
    R, _, rank, _ = bases.shape
    depth = lax.broadcasted_iota(jnp.int32, (rank, tile), 0)

    def basis(row, t):
        return split(jnp.where(depth < ranks[t * R + row], bases[row, t], 0.0))

    at = 0
    for s in range(S):
        size = (S - s) * per * rank
        src = table[2, s]
        j = s * C + src
        col_basis = basis(lax.rem(src, R), s * per + lax.div(src, R))
        half = dot3(split(weights[:, at : at + size]), col_basis, ((0,), (0,)))
        at += size
        for t in range(T):
            if t < s * per:
                out[s, t] = jnp.zeros((tile, tile), f32)
                continue
            k = t - s * per
            row = table[1, t // per]
            update = dot3(basis(row, t), split(half[k * rank : (k + 1) * rank]), ((0,), (0,)))
            out[s, t] = jnp.where(t * R + row >= j, moved[s][k] - update, 0.0)


def updates(table, ranks, weights, everyone, moved, C, per):
    R, T, rank, wide = everyone.shape
    S, tile = T // per, moved[0].shape[1]
    smem = pl.BlockSpec(memory_space=pltpu.SMEM)
    whole = lambda a: pl.BlockSpec(a.shape, lambda i: (0,) * a.ndim)
    out = jax.ShapeDtypeStruct((S, T, tile, tile), f32)
    picked = pl.BlockSpec((R, T, rank, tile), lambda i: (0, 0, 0, wide // tile - 1))
    return pl.pallas_call(
        lambda *refs: update_kernel(per, C, *refs),
        grid=(1,),
        in_specs=[smem, smem, whole(weights), picked] + [whole(m) for m in moved],
        out_specs=whole(out),
        out_shape=out,
        name="updates",
    )(table, ranks, weights, everyone, *moved)


def per_device(
    contribution,
    parent_tiles,
    row_basis,
    pivot_basis,
    tile_ranks,
    block_map,
    panel_start,
    pivot_inverse,
):
    R = lax.axis_size("row")
    C = lax.axis_size("col")
    my_row = lax.axis_index("row")
    my_col = lax.axis_index("col")
    T, S = contribution.shape[0], contribution.shape[2]
    tile = contribution.shape[4]
    rows, bcols = parent_tiles.shape[0], parent_tiles.shape[2]
    rank = row_basis.shape[2]
    width = pivot_basis.shape[3]
    per = C // R
    span = rows // S
    block = jnp.arange(S, dtype=jnp.int32)
    shift = block_map.reshape(S, C)[:, 0] - 2 * C * block
    src_row = lax.rem(my_row + C * R - shift, jnp.full_like(shift, R))
    src_col = lax.rem(my_col + C - shift, jnp.full_like(shift, C))
    row_shift = lax.rem(shift, jnp.full_like(shift, R))

    child = contribution[:, 0, :, 0]
    by_row = [rotate(child[u * per : (u + 1) * per, : u + 1], "row", row_shift[u]) for u in range(S)]

    start = panel_start[0]
    own_b = jnp.minimum((start + (my_col - start) % C) // C, bcols - 1)
    subs = R // PANEL_T
    piece = rows // per // subs
    members = C // PANEL_T
    my_member = my_col // PANEL_T

    def exchange(pieces):
        held = lax.dynamic_index_in_dim(pieces, my_member, axis=0, keepdims=False)
        for k in range(1, members):
            gone = lax.dynamic_index_in_dim(pieces, (my_member + k) % members, axis=0, keepdims=False)
            came = lax.ppermute(gone, "col", [(d, (d + PANEL_T * k) % C) for d in range(C)])
            theirs = (my_col - PANEL_T * k - start) % C < PANEL_T
            held = jnp.where(theirs, came, held)
        return held

    column = lax.dynamic_index_in_dim(parent_tiles[:, 0, :, 0], own_b, axis=1, keepdims=False)
    column = column.reshape(subs, piece, per, tile, tile)
    column = jnp.moveaxis(column, 2, 0).reshape(members, piece, tile, tile)

    factors = jnp.concatenate([pivot_basis[:, 0], row_basis[:, 0]], axis=2)
    column, factors = lax.optimization_barrier((column, factors))
    held_parent = exchange(column)
    everyone = row_gather(factors)
    everyone, by_row, held_parent = lax.optimization_barrier((everyone, by_row, held_parent))
    moved = [
        rotate(jnp.concatenate([by_row[u][:, s] for u in range(s, S)], axis=0), "col", shift[s])
        for s in range(S)
    ]
    routes = jnp.stack([shift, src_row, src_col])
    partial = products(routes, everyone, C, per, tile)
    weights = ring_sum(partial)
    payload = updates(routes, tile_ranks, weights, everyone, moved, C, per)

    first_row = lax.div(2 * C * block + shift + src_row, jnp.full_like(shift, R))
    a = jnp.arange(rows, dtype=jnp.int32)
    p_of = a - jnp.repeat(first_row, span)
    u_of = a // span
    place = jnp.where((p_of >= 0) & (p_of < per), u_of * per + p_of, -1).astype(jnp.int32)
    target_col = lax.div(2 * C * block + shift + src_col, jnp.full_like(shift, C))
    b = jnp.arange(bcols, dtype=jnp.int32)
    col_hit = (jnp.repeat(target_col, bcols // S) == b).astype(jnp.int32)

    child_col = lax.dynamic_index_in_dim(payload, own_b // (bcols // S), axis=0, keepdims=False)
    child_col = child_col.reshape(S, per, tile, tile)
    parity = jnp.arange(per, dtype=jnp.int32)
    holds = (parity[:, None] - first_row[None, :]) % per
    compact = jnp.zeros((per, S, tile, tile), f32)
    for p in range(per):
        compact = compact + jnp.where((holds == p)[:, :, None, None], child_col[None, :, p], 0.0)
    hit = lax.dynamic_index_in_dim(col_hit, own_b, axis=0, keepdims=False) > 0
    compact = jnp.where(hit, compact, 0.0).reshape(members, S // subs, tile, tile)
    held_child = exchange(compact)
    piece_rows = (my_member % subs * piece + jnp.arange(piece, dtype=jnp.int32)) * per + my_member // subs
    landed = jnp.repeat(held_child, span // per, axis=0)
    held = held_parent + jnp.where((place[piece_rows] >= 0)[:, None, None], landed, 0.0)
    panel, cols = gather_panel(held)
    panel = panel.reshape(per, subs, PANEL_T, piece, tile, tile)
    local = lax.dynamic_index_in_dim(panel, my_col // R, axis=0, keepdims=False)
    cols = jnp.where(my_row == my_col % R, local, cols.reshape(local.shape))
    cols = jnp.transpose(cols, (0, 2, 3, 1, 4)).reshape(bcols * tile, PANEL_T * tile)
    inverse = pivot_inverse.reshape(PANEL_T, tile, PANEL_T, tile)
    inverse = jnp.roll(inverse, (start % PANEL_T, start % PANEL_T), axis=(0, 2))
    inverse = inverse.reshape(PANEL_T * tile, PANEL_T * tile)
    scalars = jnp.stack([my_row, R + 0 * my_row, my_col, C + 0 * my_row, start + PANEL_T]).astype(jnp.int32)
    pad = lambda v: jnp.concatenate([v, jnp.zeros((rows - v.shape[0],), jnp.int32)])
    table = jnp.stack([pad(scalars), place, pad(col_hit)])
    return finish(table, parent_tiles, payload, panel, split_outside(inverse), split_outside(cols))


def solution(mesh):
    placed = (
        P(None, "row", None, "col", None, None),
        P(None, "row", None, "col", None, None),
        P(None, "row", None, None),
        P(None, "row", None, "col"),
        P(),
        P(),
        P(),
        P(),
    )
    return jax.shard_map(
        per_device,
        mesh=mesh,
        in_specs=placed,
        out_specs=P(None, "row", None, "col", None, None),
        check_vma=False,
    )
```
